32 devices in a mesh: dp: 16 (over z, x, core), head: 2 (over y).
Axes of the slice: x: 2, y: 2, z: 4, core: 2. Of those that a mesh axis runs over, the one named last changes fastest.
Arguments:
- tokens: bfloat16 [16, 2, 512, 1024], P('dp', None, 'head'), may hold values from -6 to 6
- out_grad: bfloat16 [16, 2, 512, 1024], P('dp', None, 'head'), may hold values from -6 to 6
- init_state: bfloat16 [16, 2, 512, 1024], P('dp', None, 'head'), may hold values from -6 to 6
- state_grad: bfloat16 [16, 2, 512, 1024], P('dp', None, 'head'), may hold values from -6 to 6
- seq_blocks: int32 [16, 2], P('dp'), may hold values from 0 to 2, as said below
- bucket_table: int32 [512], replicated, may hold values from 0 to 31, as said below
- gain_tok: float32 [1024], replicated, may hold values from 0.5 to 1.5
- gain_state: float32 [1024], replicated, may hold values from 0.5 to 1.5
- gain_mlp: float32 [1024], replicated, may hold values from 0.5 to 1.5
- query_tok: bfloat16 [1024, 1024], P(None, 'head'), may hold values from -0.1875 to 0.1875
- query_state: bfloat16 [1024, 1024], P(None, 'head'), may hold values from -0.1875 to 0.1875
- key_weight: bfloat16 [1024, 1024], P(None, 'head'), may hold values from -0.1875 to 0.1875
- value_weight: bfloat16 [1024, 1024], P(None, 'head'), may hold values from -0.1875 to 0.1875
- out_tok: bfloat16 [2, 1024, 1024], P(None, 'head'), may hold values from -1 to 1
- out_state: bfloat16 [2, 1024, 1024], P(None, 'head'), may hold values from -1 to 1
- mlp_in: bfloat16 [1024, 4096], P(None, 'head'), may hold values from -0.1875 to 0.1875
- mlp_out: bfloat16 [4096, 1024], P('head'), may hold values from -0.09375 to 0.09375
- gate_forget: float32 [1024], replicated, may hold values from -2 to 3
- gate_input: float32 [1024], replicated, may hold values from -2 to 2
- rel_bias: float32 [32, 8], P(None, 'head'), may hold values from -4 to 4
Outputs:
- new_tokens: bfloat16 [16, 2, 512, 1024], P('dp', None, 'head')
- next_state: float32 [16, 2, 512, 1024], P('dp', None, 'head')
- token_grad: float32 [16, 2, 512, 1024], P('dp', None, 'head')
- init_grad: float32 [16, 2, 512, 1024], P('dp', None, 'head')
- gain_tok_grad: float32 [1024], replicated
- gain_state_grad: float32 [1024], replicated
- gain_mlp_grad: float32 [1024], replicated
- query_tok_grad: float32 [1024, 1024], P(None, 'head')
- query_state_grad: float32 [1024, 1024], P(None, 'head')
- key_grad: float32 [1024, 1024], P(None, 'head')
- value_grad: float32 [1024, 1024], P(None, 'head')
- out_tok_grad: float32 [2, 1024, 1024], P(None, 'head')
- out_state_grad: float32 [2, 1024, 1024], P(None, 'head')
- mlp_in_grad: float32 [1024, 4096], P(None, 'head')
- mlp_out_grad: float32 [4096, 1024], P('head')
- gate_forget_grad: float32 [1024], replicated
- gate_input_grad: float32 [1024], replicated
- rel_bias_grad: float32 [32, 8], P(None, 'head')
The draws below stay inside these ranges and needn't reach their ends.
Inputs may be any that keep to these rules, and one draw needn't show every extreme that they name: `seq_blocks`: A group's first slot has 2 or 1 blocks; its second slot has 1 block or none, and none where the first has 2; each of the three combinations occurs in every draw. `bucket_table`: never falls with the distance, is 0 at distance 0 and 31 at distance 512 - 1, and takes every bucket.
All inputs are finite; a program needn't handle non-finite values.
Results may differ from the reference program's by a relative error of at most 0.02.
Values may be sent and summed in bfloat16 or wider, within the bound.
No kernel may reach another device: no remote copies, remote signals or barrier semaphores. Data moves between devices by JAX's collectives and lax.ppermute only.
A program may use at most 320 MiB of HBM per device.

```python
import jax
import jax.numpy as jnp
from jax import lax

D = 1024
HEADS = 8
HEAD_DIM = 128
FF = 4096
WINDOW = 512
STATES = 512
BUCKETS = 32
BLOCKS = 2
GROUPS = 16


def draw_seq_blocks(key, part):
    pattern = jax.random.permutation(key, GROUPS) % 3
    first_slot = jnp.where(pattern == 0, BLOCKS, BLOCKS // 2)
    second = jnp.where(pattern == 1, BLOCKS // 2, 0)
    return jnp.stack([first_slot, second], 1).astype(jnp.int32)


def draw_bucket_table(key, part):
    shuffled = jax.random.permutation(key, WINDOW - 1) + 1
    bounds = jnp.sort(shuffled[:BUCKETS - 1])
    distance = jnp.arange(WINDOW, dtype=jnp.int32)
    return jnp.sum((bounds[None, :] <= distance[:, None]).astype(jnp.int32), 1).astype(jnp.int32)


def levels(own_key, shape, shards, least, largest):
    loudness, own = 1.0, jax.random.fold_in(own_key, 6)
    for dim, parts in shards:
        heights = jnp.exp(jax.random.uniform(jax.random.fold_in(own, dim), (parts,), jnp.float32, least / len(shards), largest / len(shards)))
        loudness = loudness * jnp.repeat(heights, shape[dim] // parts).reshape([-1 if axis == dim else 1 for axis in range(len(shape))])
    return loudness


def normal_values(rng, dims, width, most, shards=(), held_as=jnp.bfloat16):
    factor_of = levels(rng, dims, shards, -0.22, 0.18) if shards else 1.0
    array = jax.random.normal(rng, dims, jnp.float32) * width * factor_of
    return jnp.minimum(jnp.maximum(array, -most), most).astype(held_as)


def setup_inputs(seed: int = 0) -> dict:
    seeds = jax.random.split(jax.random.key(seed), 21)
    tokens = normal_values(seeds[0], (GROUPS, BLOCKS, WINDOW, D), 1.0, 6.0, ((0, 16), (2, 2)))
    out_grad = normal_values(seeds[1], (GROUPS, BLOCKS, WINDOW, D), 1.0, 6.0, ((0, 16), (2, 2)))
    init_state = normal_values(seeds[2], (GROUPS, 2, STATES, D), 1.0, 6.0, ((0, 16), (2, 2)))
    state_grad = normal_values(seeds[3], (GROUPS, 2, STATES, D), 1.0, 6.0, ((0, 16), (2, 2)))
    seq_blocks = draw_seq_blocks(jax.random.fold_in(seeds[20], 71), 0)
    bucket_table = draw_bucket_table(jax.random.fold_in(seeds[20], 71), 0)
    gain_tok = jnp.clip(1.0 + 0.1 * jax.random.normal(seeds[6], (D,), jnp.float32), 0.5, 1.5)
    gain_state = jnp.clip(1.0 + 0.1 * jax.random.normal(seeds[7], (D,), jnp.float32), 0.5, 1.5)
    gain_mlp = jnp.clip(1.0 + 0.1 * jax.random.normal(seeds[8], (D,), jnp.float32), 0.5, 1.5)
    query_tok = normal_values(seeds[9], (D, D), D ** -0.5, 0.1875, ((1, 2),))
    query_state = normal_values(seeds[10], (D, D), D ** -0.5, 0.1875, ((1, 2),))
    key_weight = normal_values(seeds[11], (D, D), D ** -0.5, 0.1875, ((1, 2),))
    value_weight = normal_values(seeds[12], (D, D), D ** -0.5, 0.1875, ((1, 2),))
    out_tok = normal_values(seeds[13], (2, D, D), 32 ** -0.5, 1.0, ((1, 2),))
    out_state = normal_values(seeds[14], (2, D, D), 32 ** -0.5, 1.0, ((1, 2),))
    mlp_in = normal_values(seeds[15], (D, FF), D ** -0.5, 0.1875, ((1, 2),))
    mlp_out = normal_values(seeds[16], (FF, D), FF ** -0.5, 0.09375, ((0, 2),))
    gate_forget = jnp.clip(jax.random.uniform(seeds[17], (D,), jnp.float32, -2.0, 3.0), -2.0, 3.0)
    gate_input = jnp.clip(jax.random.uniform(seeds[18], (D,), jnp.float32, -2.0, 2.0), -2.0, 2.0)
    rel_bias = normal_values(seeds[19], (BUCKETS, HEADS), 1.0, 4.0, ((1, 2),), jnp.float32)
    return dict(tokens=tokens, out_grad=out_grad, init_state=init_state, state_grad=state_grad, seq_blocks=seq_blocks, bucket_table=bucket_table, gain_tok=gain_tok, gain_state=gain_state, gain_mlp=gain_mlp, query_tok=query_tok, query_state=query_state, key_weight=key_weight, value_weight=value_weight, out_tok=out_tok, out_state=out_state, mlp_in=mlp_in, mlp_out=mlp_out, gate_forget=gate_forget, gate_input=gate_input, rel_bias=rel_bias)


@jax.custom_vjp
def low(v):
    return lax.optimization_barrier(v.astype(jnp.bfloat16)).astype(jnp.float32)

@jax.custom_vjp
def low_back(v):
    return v

def low_keep(v):
    return (low(v), None)

def low_pass(kept, grad):
    return (grad,)

def back_keep(v):
    return (v, None)

def back_low(kept, grad):
    return (low(grad),)
low.defvjp(low_keep, low_pass)
low_back.defvjp(back_keep, back_low)
EPSILON = 1e-05
MASKED = -1e+30

def both_round(values):
    return low_back(low(values))

def mat_dot(left_side, right_side):
    return jnp.dot(left_side, right_side, precision=lax.Precision.HIGHEST)

def layer_norm(values, scale_row):
    centred = values - lax.optimization_barrier(jnp.mean(values, axis=-1, keepdims=True))
    variance = lax.optimization_barrier(jnp.mean(centred * centred, axis=-1, keepdims=True))
    return centred * lax.rsqrt(variance + EPSILON) * scale_row

def split_heads(matrix):
    return matrix.reshape(matrix.shape[0], HEADS, HEAD_DIM)

def attend(queries, key_rows, value_rows, score_bias, allowed):
    scores = jnp.einsum('qhe,khe->hqk', queries, key_rows, precision=lax.Precision.HIGHEST) * HEAD_DIM ** (-0.5) + score_bias
    scores = jnp.where(allowed, low_back(scores), MASKED)
    weights = low(jax.nn.softmax(scores, axis=-1))
    return both_round(jnp.einsum('hqk,khe->qhe', weights, value_rows, precision=lax.Precision.HIGHEST))

def recurrent_block(params, token_rows, state_in, key_prev, value_prev, allowed, bias_full):
    gain_tok, gain_state, gain_mlp, query_tok, query_state, key_weight, value_weight, out_tok, out_state, mlp_in, mlp_out, gate_forget, gate_input, rel_bias = params
    normed = low(layer_norm(token_rows, gain_tok))
    normed_state = low(layer_norm(state_in, gain_state))
    q_tok = both_round(mat_dot(normed, query_tok))
    k_tok = both_round(mat_dot(normed, key_weight))
    v_tok = both_round(mat_dot(normed, value_weight))
    q_state = both_round(mat_dot(normed_state, query_state))
    k_state = both_round(mat_dot(normed_state, key_weight))
    v_state = both_round(mat_dot(normed_state, value_weight))
    key_window = jnp.concatenate([key_prev, k_tok], 0)
    value_window = jnp.concatenate([value_prev, v_tok], 0)
    self_out = attend(split_heads(q_tok), split_heads(key_window), split_heads(value_window), bias_full, allowed)
    cross_out = attend(split_heads(q_tok), split_heads(k_state), split_heads(v_state), 0.0, True)
    state_self = attend(split_heads(q_state), split_heads(k_state), split_heads(v_state), 0.0, True)
    state_cross = attend(split_heads(q_state), split_heads(k_tok), split_heads(v_tok), 0.0, True)
    row_count = token_rows.shape[0]
    state_count = state_in.shape[0]
    tok_branch = low_back(mat_dot(self_out.reshape(row_count, D), out_tok[0]) + mat_dot(cross_out.reshape(row_count, D), out_tok[1]))
    update = low_back(mat_dot(state_self.reshape(state_count, D), out_state[0]) + mat_dot(state_cross.reshape(state_count, D), out_state[1]))
    mid_rows = token_rows + tok_branch
    normed_mid = low(layer_norm(mid_rows, gain_mlp))
    hidden_pre = low_back(mat_dot(normed_mid, mlp_in))
    hidden = low(jax.nn.gelu(hidden_pre, approximate=True))
    new_rows = mid_rows + low_back(mat_dot(hidden, mlp_out))
    new_state = jax.nn.sigmoid(gate_forget) * state_in + jax.nn.sigmoid(gate_input) * update
    return (new_rows, new_state, k_tok, v_tok)

def group_forward(params, token_blocks, states, lengths, bucket_table):
    rel_bias = params[13]
    first_len = lengths[0]
    all_len = lengths[0] + lengths[1]
    row_index = jnp.arange(WINDOW, dtype=jnp.int32)
    col_index = jnp.arange(2 * WINDOW, dtype=jnp.int32)
    distance = WINDOW + row_index[:, None] - col_index[None, :]
    window_inside = (distance >= 0) & (distance < WINDOW)
    current_cols = (col_index >= WINDOW)[None, :]
    bias_full = jnp.transpose(rel_bias[bucket_table[jnp.clip(distance, 0, WINDOW - 1)]], (2, 0, 1))

    def block_step(carried, inputs):
        state_run, key_prev, value_prev, finals = carried
        block_rows, block_id = inputs
        is_live = block_id < all_len
        is_start = (block_id == 0) | (block_id == first_len)
        is_second = block_id >= first_len
        state_in = jnp.where(is_start, jnp.where(is_second, states[1], states[0]), state_run)
        allowed = window_inside & (current_cols | jnp.logical_not(is_start))
        new_rows, new_state, key_now, value_now = recurrent_block(params, block_rows, state_in, key_prev, value_prev, allowed, bias_full)
        out_rows = jnp.where(is_live, new_rows, block_rows)
        state_next = jnp.where(is_live, new_state, state_in)
        slot_pick = (jnp.arange(2, dtype=jnp.int32) == is_second.astype(jnp.int32)) & is_live
        finals = jnp.where(slot_pick[:, None, None], state_next[None], finals)
        return ((state_next, key_now, value_now, finals), out_rows)
    empty_keys = jnp.zeros((WINDOW, D), jnp.float32)
    start_carry = (jnp.zeros((STATES, D), jnp.float32), empty_keys, empty_keys, states)
    end_carry, out_blocks = lax.scan(jax.checkpoint(block_step), start_carry, (token_blocks, jnp.arange(BLOCKS, dtype=jnp.int32)))
    return (out_blocks, end_carry[3])

def reference(tokens, out_grad, init_state, state_grad, seq_blocks, bucket_table, gain_tok, gain_state, gain_mlp, query_tok, query_state, key_weight, value_weight, out_tok, out_state, mlp_in, mlp_out, gate_forget, gate_input, rel_bias):
    params = tuple((weight_item.astype(jnp.float32) for weight_item in (gain_tok, gain_state, gain_mlp, query_tok, query_state, key_weight, value_weight, out_tok, out_state, mlp_in, mlp_out, gate_forget, gate_input, rel_bias)))

    def per_group(totals, inputs):
        token_blocks, cot_blocks, states, state_cots, lengths = inputs

        def forward(param_list, rows_in, states_in):
            return group_forward(param_list, rows_in, states_in, lengths, bucket_table)
        outputs, pullback = jax.vjp(forward, params, token_blocks.astype(jnp.float32), states.astype(jnp.float32))
        param_grads, row_grads, state_grads = pullback((cot_blocks.astype(jnp.float32), state_cots.astype(jnp.float32)))
        totals = jax.tree.map(jnp.add, totals, param_grads)
        return (totals, (outputs[0].astype(jnp.bfloat16), outputs[1], row_grads, state_grads))
    zero_grads = tuple((jnp.zeros_like(weight_item) for weight_item in params))
    totals, results = lax.scan(per_group, zero_grads, (tokens, out_grad, init_state, state_grad, seq_blocks))
    return (results[0], results[1], results[2], results[3], totals[0], totals[1], totals[2], totals[3], totals[4], totals[5], totals[6], totals[7], totals[8], totals[9], totals[10], totals[11], totals[12], totals[13])
```

```python
import functools
import math

import jax
import jax.numpy as jnp
from jax import lax
from jax.experimental import pallas as pl
from jax.experimental.pallas import tpu as pltpu
from jax.sharding import PartitionSpec as P

HEAD_DIM = 128
WINDOW = 512
BUCKETS = 32
EPSILON = 1e-05
MASKED = -1e30
SCALE = HEAD_DIM ** (-0.5)
F32 = jnp.float32
BF16 = jnp.bfloat16
MIB = 1024 * 1024
LIVE, START, FLIP, PREV = 0, 1, 2, 3


def nn(a, b):
    return lax.dot_general(a, b, (((1,), (0,)), ((), ())), preferred_element_type=F32)


def nt(a, b):
    return lax.dot_general(a, b, (((1,), (1,)), ((), ())), preferred_element_type=F32)


def tn(a, b):
    return lax.dot_general(a, b, (((0,), (0,)), ((), ())), preferred_element_type=F32)


def nbytes(*arrays):
    return sum(math.prod(a.shape) * jnp.dtype(a.dtype).itemsize for a in arrays)


def call(body, args, outs, grid=(), in_specs=None, out_specs=None, scratch=(), prefetch=0, flops=0, name=None, vmem=48):
    whole = lambda a: pl.BlockSpec(a.shape, lambda *ids, n=len(a.shape): (0,) * n)
    arrays = args[prefetch:]
    if in_specs is None:
        in_specs = [None] * len(arrays)
    if out_specs is None:
        out_specs = [None] * len(outs)
    in_specs = [whole(a) if s is None else s for a, s in zip(arrays, in_specs)]
    out_specs = [whole(o) if s is None else s for o, s in zip(outs, out_specs)]
    return pl.pallas_call(
        body,
        out_shape=list(outs),
        grid_spec=pltpu.PrefetchScalarGridSpec(
            num_scalar_prefetch=prefetch,
            grid=grid or (1,),
            in_specs=in_specs,
            out_specs=out_specs,
            scratch_shapes=list(scratch),
        ),
        compiler_params=pltpu.CompilerParams(vmem_limit_bytes=vmem * MIB),
        cost_estimate=pl.CostEstimate(flops=int(flops), transcendentals=0, bytes_accessed=nbytes(*arrays, *outs)),
        name=name,
    )(*args)


def sds(shape, dtype):
    return jax.ShapeDtypeStruct(shape, dtype)


def norm_parts(v):
    mean = jnp.mean(v, axis=-1, keepdims=True)
    cent = v - mean
    var = jnp.mean(cent * cent, axis=-1, keepdims=True)
    inv = lax.rsqrt(var + EPSILON)
    return cent * inv, inv


def norm_back(n, inv, w, g):
    wg = w * g
    return (wg - jnp.mean(wg, -1, keepdims=True) - n * jnp.mean(wg * n, -1, keepdims=True)) * inv


def sum_refs(refs):
    total = refs[0][...].astype(F32)
    for r in refs[1:]:
        total = total + r[...].astype(F32)
    return total


def project(chunks, gain, wq, wk, wv, name):
    count = len(chunks)
    rows, d = chunks[0].shape
    w = wq.shape[1]
    tile = min(w, 256)
    total = rows * count

    def body(*refs):
        xs, (g, q_w, k_w, v_w), (n_ref, q_ref, k_ref, v_ref) = refs[:count], refs[count : count + 4], refs[count + 4 :]

        @pl.when(pl.program_id(0) == 0)
        def _():
            for c in range(count):
                x = xs[c][...]
                if gain is not None:
                    x = (norm_parts(x.astype(F32))[0] * g[...]).astype(BF16)
                n_ref[c * rows : (c + 1) * rows, :] = x

        n = n_ref[...]
        q_ref[...] = nn(n, q_w[...]).astype(BF16)
        k_ref[...] = nn(n, k_w[...]).astype(BF16)
        v_ref[...] = nn(n, v_w[...]).astype(BF16)

    g = jnp.zeros((1, d), F32) if gain is None else gain[None]
    wspec = pl.BlockSpec((d, tile), lambda i: (0, i))
    ospec = pl.BlockSpec((total, tile), lambda i: (0, i))
    out = sds((total, w), BF16)
    return call(
        body,
        [*chunks, g, wq, wk, wv],
        [sds((total, d), BF16), out, out, out],
        grid=(w // tile,),
        in_specs=[None] * (count + 1) + [wspec] * 3,
        out_specs=[None] + [ospec] * 3,
        flops=6 * total * d * w,
        name=name,
    )


def softmax_cols(s):
    e = jnp.exp(s - jnp.max(s, axis=0, keepdims=True))
    return (e * (1.0 / jnp.sum(e, axis=0, keepdims=True))).astype(BF16)


def write_parts(acc, parts, rows):
    for c, part in enumerate(parts):
        part[...] = acc[c * rows : (c + 1) * rows, :].astype(BF16)


def window_masks(flags):
    key_row = lax.broadcasted_iota(jnp.int32, (WINDOW, WINDOW), 0) ^ flags[FLIP]
    query_row = lax.broadcasted_iota(jnp.int32, (WINDOW, WINDOW), 1) ^ flags[FLIP]
    return key_row, query_row


def attend_tokens(flags, q, kc, vc, prev, ks, vs, by_dist, ow, chunks, name):
    t, w = q.shape
    d = ow.shape[2]
    heads = w // HEAD_DIM
    has_prev = prev is not None
    rows = t // chunks

    def body(flags, *refs):
        refs = list(refs)
        q_r, kc_r, vc_r = refs[:3]
        refs = refs[3:]
        if has_prev:
            kp_r, vp_r = refs[:2]
            refs = refs[2:]
        ks_r, vs_r, f_r, ow_r, so_r, co_r, ps_r, pc_r = refs[:8]
        parts, acc = refs[8:-1], refs[-1]
        h = pl.program_id(0)
        qv = q_r[...]
        key_row, query_row = window_masks(flags)
        tri = key_row <= query_row
        s = nt(kc_r[...], qv)
        if has_prev:
            s = jnp.where(tri, s, nt(kp_r[...], qv))
            allowed = key_row <= query_row + flags[PREV] * (2 * WINDOW)
        else:
            allowed = tri
        bias = pltpu.roll(jnp.broadcast_to(f_r[0], (WINDOW, WINDOW)), 0, 1, stride=1, stride_axis=0)
        p = softmax_cols(jnp.where(allowed, s * SCALE + bias, MASKED))
        ps_r[0] = p
        if has_prev:
            zero = jnp.zeros_like(p)
            o = tn(jnp.where(tri, p, zero), vc_r[...]) + tn(jnp.where(tri, zero, p), vp_r[...])
        else:
            o = tn(p, vc_r[...])
        so = o.astype(BF16)
        so_r[...] = so
        p = softmax_cols(nt(ks_r[...], qv) * SCALE)
        pc_r[0] = p
        co = tn(p, vs_r[...]).astype(BF16)
        co_r[...] = co
        term = nn(jnp.concatenate([so, co], 1), ow_r[...].reshape(2 * HEAD_DIM, d))

        @pl.when(h == 0)
        def _():
            acc[...] = term

        @pl.when(h > 0)
        def _():
            acc[...] += term

        @pl.when(h == heads - 1)
        def _():
            write_parts(acc, parts, rows)

    head = pl.BlockSpec((t, HEAD_DIM), lambda h, *_: (0, h))
    pspec = pl.BlockSpec((1, WINDOW, t), lambda h, *_: (h, 0, 0))
    args = [flags, q, kc, vc] + (list(prev) if has_prev else []) + [ks, vs, by_dist, ow]
    n_heads = 7 if has_prev else 5
    return call(
        body,
        args,
        [sds((t, w), BF16)] * 2 + [sds((heads, WINDOW, t), BF16)] * 2 + [sds((rows, d), BF16)] * chunks,
        grid=(heads,),
        in_specs=[head] * n_heads
        + [
            pl.BlockSpec((1, 1, WINDOW), lambda h, *_: (h, 0, 0)),
            pl.BlockSpec((2, HEAD_DIM, d), lambda h, *_: (0, h, 0)),
        ],
        out_specs=[head] * 2 + [pspec] * 2 + [None] * chunks,
        scratch=[pltpu.VMEM((t, d), F32)],
        prefetch=1,
        flops=heads * (2 * t * t * HEAD_DIM * (6 if has_prev else 4) + 4 * t * HEAD_DIM * d),
        name=name,
    )


def attend_states(q, ks, vs, kt, vt, ow, chunks, name):
    t, w = q.shape
    d = ow.shape[2]
    heads = w // HEAD_DIM
    rows = t // chunks

    def body(q_r, ks_r, vs_r, kt_r, vt_r, ow_r, so_r, co_r, ps_r, pc_r, *rest):
        parts, acc = rest[:-1], rest[-1]
        h = pl.program_id(0)
        qv = q_r[...]
        p = softmax_cols(nt(ks_r[...], qv) * SCALE)
        ps_r[0] = p
        so = tn(p, vs_r[...]).astype(BF16)
        so_r[...] = so
        p = softmax_cols(nt(kt_r[...], qv) * SCALE)
        pc_r[0] = p
        co = tn(p, vt_r[...]).astype(BF16)
        co_r[...] = co
        term = nn(jnp.concatenate([so, co], 1), ow_r[...].reshape(2 * HEAD_DIM, d))

        @pl.when(h == 0)
        def _():
            acc[...] = term

        @pl.when(h > 0)
        def _():
            acc[...] += term

        @pl.when(h == heads - 1)
        def _():
            write_parts(acc, parts, rows)

    head = pl.BlockSpec((t, HEAD_DIM), lambda h: (0, h))
    pspec = pl.BlockSpec((1, ks.shape[0], t), lambda h: (h, 0, 0))
    return call(
        body,
        [q, ks, vs, kt, vt, ow],
        [sds((t, w), BF16)] * 2 + [sds((heads, ks.shape[0], t), BF16)] * 2 + [sds((rows, d), BF16)] * chunks,
        grid=(heads,),
        in_specs=[head] * 5 + [pl.BlockSpec((2, HEAD_DIM, d), lambda h: (0, h, 0))],
        out_specs=[head] * 2 + [pspec] * 2 + [None] * chunks,
        scratch=[pltpu.VMEM((t, d), F32)],
        flops=heads * (8 * t * t * HEAD_DIM + 4 * t * HEAD_DIM * d),
        name=name,
    )


def score_back(p16, dp):
    p = p16.astype(F32)
    t = p * dp
    return (t - p * jnp.sum(t, axis=0, keepdims=True)).astype(BF16)


def distance_sums(ds):
    x = ds.astype(F32)
    n = WINDOW
    while n > 1:
        n //= 2
        x = x[:n] + pltpu.roll(x[n:], WINDOW - n, 1)
    return x


def out_grads(branch_refs, ow_r, d):
    w2 = ow_r[...].reshape(2 * HEAD_DIM, d)
    return jnp.concatenate([nt(b[...], w2).astype(BF16) for b in branch_refs], 0)


def attend_tokens_back(flags, q, kc, vc, prev, ks, vs, ps, pc, branch, ow, adds, final, name):
    t, w = q.shape
    d = ow.shape[2]
    heads = w // HEAD_DIM
    has_prev = prev is not None
    count = len(branch)
    given = [a for a in adds if a is not None]

    def body(flags, *refs):
        refs = list(refs)
        q_r, kc_r, vc_r = refs[:3]
        refs = refs[3:]
        if has_prev:
            kp_r, vp_r = refs[:2]
            refs = refs[2:]
        ks_r, vs_r, ps_r, pc_r = refs[:4]
        br = refs[4 : 4 + count]
        ow_r = refs[4 + count]
        refs = refs[5 + count :]
        add_refs = []
        for a in adds:
            add_refs.append(None if a is None else refs.pop(0))
        dq_r, dkc_r, dvc_r, dks_r, dvs_r, bd_r = refs[:6]
        do = out_grads(br, ow_r, d)
        do_s, do_c = do[:, :HEAD_DIM], do[:, HEAD_DIM:]
        qv = q_r[...]

        def put(ref, value, add):
            if add is not None:
                value = value + add[...].astype(F32)
            ref[...] = value.astype(ref.dtype)

        p16 = ps_r[0]
        dp = nt(vc_r[...], do_s)
        if has_prev:
            key_row, query_row = window_masks(flags)
            tri = key_row <= query_row
            dp = jnp.where(tri, dp, nt(vp_r[...], do_s))
        ds = score_back(p16, dp)
        bd_r[0] = distance_sums(ds)
        if has_prev:
            zero = jnp.zeros_like(ds)
            p_prev, ds_prev = jnp.where(tri, zero, p16), jnp.where(tri, zero, ds)
            p16, ds = jnp.where(tri, p16, zero), jnp.where(tri, ds, zero)
            refs[7][...] = nn(p_prev, do_s)
            refs[6][...] = nn(ds_prev, qv) * SCALE
        put(dvc_r, nn(p16, do_s), add_refs[1])
        put(dkc_r, nn(ds, qv) * SCALE, add_refs[0])
        dq = tn(ds, kc_r[...])
        if has_prev:
            dq = dq + tn(ds_prev, kp_r[...])
        p16 = pc_r[0]
        ds = score_back(p16, nt(vs_r[...], do_c))
        put(dvs_r, nn(p16, do_c), add_refs[3])
        put(dks_r, nn(ds, qv) * SCALE, add_refs[2])
        dq = dq + tn(ds, ks_r[...])
        dq_r[...] = (dq * SCALE).astype(BF16)

    head = pl.BlockSpec((t, HEAD_DIM), lambda h, *_: (0, h))
    pspec = pl.BlockSpec((1, WINDOW, t), lambda h, *_: (h, 0, 0))
    args = [flags, q, kc, vc] + (list(prev) if has_prev else []) + [ks, vs, ps, pc, *branch, ow, *given]
    n_heads = 7 if has_prev else 5
    full = lambda dt: sds((t, w), dt)
    outs = [full(BF16), full(final[0]), full(final[0]), full(final[1]), full(final[1]), sds((heads, 1, WINDOW), F32)]
    out_specs = [head] * 5 + [pl.BlockSpec((1, 1, WINDOW), lambda h, *_: (h, 0, 0))]
    if has_prev:
        outs += [full(F32)] * 2
        out_specs += [head] * 2
    return call(
        body,
        args,
        outs,
        grid=(heads,),
        in_specs=[head] * n_heads
        + [pspec] * 2
        + [None] * count
        + [pl.BlockSpec((2, HEAD_DIM, d), lambda h, *_: (0, h, 0))]
        + [head] * len(given),
        out_specs=out_specs,
        prefetch=1,
        flops=heads * (2 * t * t * HEAD_DIM * (12 if has_prev else 8) + 4 * t * HEAD_DIM * d),
        name=name,
    )


def attend_states_back(q, ks, vs, kt, vt, ps, pc, update_grad, ow, adds, final, name):
    t, w = q.shape
    d = ow.shape[2]
    heads = w // HEAD_DIM
    count = len(update_grad)
    given = [a for a in adds if a is not None]

    def body(*refs):
        refs = list(refs)
        q_r, ks_r, vs_r, kt_r, vt_r, ps_r, pc_r = refs[:7]
        br = refs[7 : 7 + count]
        ow_r = refs[7 + count]
        refs = refs[8 + count :]
        add_refs = []
        for a in adds:
            add_refs.append(None if a is None else refs.pop(0))
        dq_r, dkt_r, dvt_r, dks_r, dvs_r = refs
        do = out_grads(br, ow_r, d)
        do_s, do_c = do[:, :HEAD_DIM], do[:, HEAD_DIM:]
        qv = q_r[...]

        def put(ref, value, add):
            if add is not None:
                value = value + add[...].astype(F32)
            ref[...] = value.astype(ref.dtype)

        p16 = ps_r[0]
        ds = score_back(p16, nt(vs_r[...], do_s))
        put(dvs_r, nn(p16, do_s), add_refs[3])
        put(dks_r, nn(ds, qv) * SCALE, add_refs[2])
        dq = tn(ds, ks_r[...])
        p16 = pc_r[0]
        ds = score_back(p16, nt(vt_r[...], do_c))
        put(dvt_r, nn(p16, do_c), add_refs[1])
        put(dkt_r, nn(ds, qv) * SCALE, add_refs[0])
        dq = dq + tn(ds, kt_r[...])
        dq_r[...] = (dq * SCALE).astype(BF16)

    head = pl.BlockSpec((t, HEAD_DIM), lambda h: (0, h))
    pspec = pl.BlockSpec((1, ks.shape[0], t), lambda h: (h, 0, 0))
    full = lambda dt: sds((t, w), dt)
    return call(
        body,
        [q, ks, vs, kt, vt, ps, pc, *update_grad, ow, *given],
        [full(BF16), full(final[0]), full(final[0]), full(final[1]), full(final[1])],
        grid=(heads,),
        in_specs=[head] * 5
        + [pspec] * 2
        + [None] * count
        + [pl.BlockSpec((2, HEAD_DIM, d), lambda h: (0, h, 0))]
        + [head] * len(given),
        out_specs=[head] * 5,
        flops=heads * (16 * t * t * HEAD_DIM + 4 * t * HEAD_DIM * d),
        name=name,
    )


def project_back(dq, dk, dv, wq, wk, wv, chunks, name):
    t, w = dq.shape
    d = wq.shape[0]
    tile = min(d, 512)
    rows = t // chunks

    def body(dq_r, dk_r, dv_r, wq_r, wk_r, wv_r, *parts):
        total = nt(dq_r[...], wq_r[...]) + nt(dk_r[...], wk_r[...]) + nt(dv_r[...], wv_r[...])
        write_parts(total, parts, rows)

    wspec = pl.BlockSpec((tile, w), lambda i: (i, 0))
    return call(
        body,
        [dq, dk, dv, wq, wk, wv],
        [sds((rows, d), BF16)] * chunks,
        grid=(d // tile,),
        in_specs=[None] * 3 + [wspec] * 3,
        out_specs=[pl.BlockSpec((rows, tile), lambda i: (0, i))] * chunks,
        flops=6 * t * d * w,
        name=name,
    )


def feed_forward(normed, cots, w_in, w_out, name):
    count = len(normed)
    rows, d = normed[0].shape
    f = w_in.shape[1]
    tile = min(f, 512)
    t = rows * count
    c0 = math.sqrt(2.0 / math.pi)

    def body(*refs):
        nm, og = refs[:count], refs[count : 2 * count]
        wi_r, wo_r, hid_r, pre_r = refs[2 * count : 2 * count + 4]
        rest = refs[2 * count + 4 :]
        parts_y, parts_g, acc_y, acc_g = rest[:count], rest[count : 2 * count], rest[-2], rest[-1]
        i = pl.program_id(0)
        wi, wo = wi_r[...], wo_r[...]
        for c in range(count):
            at = slice(c * rows, (c + 1) * rows)
            v = nn(nm[c][...], wi)
            sq = v * v
            th = jnp.tanh(v * (c0 + c0 * 0.044715 * sq))
            half = 0.5 + 0.5 * th
            hidden = (v * half).astype(BF16)
            slope = half + (0.5 * v) * (1.0 - th * th) * (c0 + 3.0 * c0 * 0.044715 * sq)
            hid_r[at, :] = hidden
            pre = (nt(og[c][...], wo) * slope).astype(BF16)
            pre_r[at, :] = pre
            y = nn(hidden, wo)
            g = nt(pre, wi)

            @pl.when(i == 0)
            def _():
                acc_y[at, :] = y
                acc_g[at, :] = g

            @pl.when(i > 0)
            def _():
                acc_y[at, :] += y
                acc_g[at, :] += g

        @pl.when(i == f // tile - 1)
        def _():
            write_parts(acc_y, parts_y, rows)
            write_parts(acc_g, parts_g, rows)

    hspec = pl.BlockSpec((t, tile), lambda i: (0, i))
    return call(
        body,
        [*normed, *cots, w_in, w_out],
        [sds((t, f), BF16)] * 2 + [sds((rows, d), BF16)] * (2 * count),
        grid=(f // tile,),
        in_specs=[None] * (2 * count)
        + [pl.BlockSpec((d, tile), lambda i: (0, i)), pl.BlockSpec((tile, d), lambda i: (i, 0))],
        out_specs=[hspec] * 2 + [None] * (2 * count),
        scratch=[pltpu.VMEM((t, d), F32)] * 2,
        flops=8 * t * d * f,
        name=name,
    )


def mid_norm(tok, adds, gain, name):
    def body(tok_r, g_r, *refs):
        adds_r, (mid_r, nm_r) = refs[:-2], refs[-2:]
        mid = tok_r[...].astype(F32) + sum_refs(adds_r)
        mid_r[...] = mid
        nm_r[...] = (norm_parts(mid)[0] * g_r[...]).astype(BF16)

    return call(body, [tok, gain[None], *adds], [sds(tok.shape, F32), sds(tok.shape, BF16)], name=name)


def state_step(flags, first, second, adds, forget, admit, gain, name):
    def body(flags, a_r, b_r, f_r, i_r, g_r, *refs):
        adds_r, (upd_r, car_r, st_r, n_r) = refs[:-4], refs[-4:]
        upd = sum_refs(adds_r)
        upd_r[...] = upd
        car = jax.nn.sigmoid(f_r[...]) * a_r[...].astype(F32) + jax.nn.sigmoid(i_r[...]) * upd
        car_r[...] = car
        pick = flags[START].astype(F32)
        st = jnp.where(pick > 0.5, b_r[...].astype(F32), car)
        st_r[...] = st
        n_r[...] = (norm_parts(st)[0] * g_r[...]).astype(BF16)

    full = sds(first.shape, F32)
    return call(
        body,
        [flags, first, second, forget[None], admit[None], gain[None], *adds],
        [full, full, full, sds(first.shape, BF16)],
        prefetch=1,
        name=name,
    )


def mid_back(mid, gain, cot, adds, name):
    def body(mid_r, g_r, cot_r, *refs):
        adds_r, (mg_r, mg16_r, gg_r) = refs[:-3], refs[-3:]
        n, inv = norm_parts(mid_r[...])
        g = sum_refs(adds_r)
        mg = cot_r[...].astype(F32) + norm_back(n, inv, g_r[...], g)
        mg_r[...] = mg
        mg16_r[...] = mg.astype(BF16)
        gg_r[...] = jnp.sum(g * n, 0, keepdims=True)

    return call(
        body,
        [mid, gain[None], cot, *adds],
        [sds(mid.shape, F32), sds(mid.shape, BF16), sds((1, mid.shape[1]), F32)],
        name=name,
    )


def token_back(flags, live_at, tok, gain, mg, cot, adds, name):
    def body(flags, tok_r, g_r, mg_r, cot_r, *refs):
        adds_r, (row_r, gg_r) = refs[:-2], refs[-2:]
        n, inv = norm_parts(tok_r[...].astype(F32))
        g = sum_refs(adds_r)
        row = mg_r[...] + norm_back(n, inv, g_r[...], g)
        if live_at is not None:
            row = jnp.where(flags[live_at].astype(F32) > 0.5, row, cot_r[...].astype(F32))
        row_r[...] = row
        gg_r[...] = jnp.sum(g * n, 0, keepdims=True)

    return call(
        body,
        [flags, tok, gain[None], mg, cot, *adds],
        [sds(tok.shape, F32), sds((1, tok.shape[1]), F32)],
        prefetch=1,
        name=name,
    )


def gate_terms(snc, upd, state, f_r, i_r):
    sf, si = jax.nn.sigmoid(f_r[...]), jax.nn.sigmoid(i_r[...])
    return (
        sf,
        si,
        jnp.sum(snc * state, 0, keepdims=True) * (sf * (1.0 - sf)),
        jnp.sum(snc * upd, 0, keepdims=True) * (si * (1.0 - si)),
    )


def state_back_second(flags, state, gain, cot0, cot1, upd, forget, admit, adds, name):
    def body(flags, st_r, g_r, c0_r, c1_r, upd_r, f_r, i_r, *refs):
        adds_r, (ig_r, snc0_r, ug_r, gg_r, gf_r, gi_r) = refs[:-6], refs[-6:]
        live = flags[LIVE].astype(F32)
        start = flags[START].astype(F32)
        c0, c1 = c0_r[...].astype(F32), c1_r[...].astype(F32)
        snc = jnp.where(start > 0.5, c1, c0) * live
        st = st_r[...]
        n, inv = norm_parts(st)
        g = sum_refs(adds_r)
        sf, si, gf, gi = gate_terms(snc, upd_r[...], st, f_r, i_r)
        back = jnp.where(live > 0.5, sf * snc + norm_back(n, inv, g_r[...], g), snc)
        ig_r[...] = jnp.where(start * live > 0.5, back, c1)
        snc0 = jnp.where(start > 0.5, c0, back)
        snc0_r[...] = snc0
        ug_r[...] = (si * snc0).astype(BF16)
        gg_r[...] = jnp.sum(g * n, 0, keepdims=True)
        gf_r[...] = gf
        gi_r[...] = gi

    full, row = sds(state.shape, F32), sds((1, state.shape[1]), F32)
    return call(
        body,
        [flags, state, gain[None], cot0, cot1, upd, forget[None], admit[None], *adds],
        [full, full, sds(state.shape, BF16), row, row, row],
        prefetch=1,
        name=name,
    )


def state_back_first(state, gain, snc, upd, forget, admit, adds, name):
    def body(st_r, g_r, snc_r, upd_r, f_r, i_r, *refs):
        adds_r, (ig_r, gg_r, gf_r, gi_r) = refs[:-4], refs[-4:]
        st = st_r[...].astype(F32)
        n, inv = norm_parts(st)
        g = sum_refs(adds_r)
        snc = snc_r[...]
        sf, _, gf, gi = gate_terms(snc, upd_r[...], st, f_r, i_r)
        ig_r[...] = sf * snc + norm_back(n, inv, g_r[...], g)
        gg_r[...] = jnp.sum(g * n, 0, keepdims=True)
        gf_r[...] = gf
        gi_r[...] = gi

    full, row = sds(state.shape, F32), sds((1, state.shape[1]), F32)
    return call(
        body,
        [state, gain[None], snc, upd, forget[None], admit[None], *adds],
        [full, row, row, row],
        name=name,
    )


def piece_positions(index, size, order):
    rel = jnp.arange(size, dtype=jnp.int32) ^ index
    pos = jnp.zeros((size,), jnp.int32)
    for bit in order:
        pos = pos * 2 + ((rel >> bit) & 1)
    return pos


def weight_grad(table, lhs, rhs, size, name):
    n = rhs[0].shape[1]
    groups = len(lhs)
    mg = lhs[0][0].shape[1]
    m = mg * groups
    piece = m // size
    tile = min(mg, 256)
    per = tile // piece
    half = size // 2
    k_lhs, k_rhs = len(lhs[0]), len(rhs)
    steps = mg // tile

    def body(table, *refs):
        l_refs, r_refs = refs[: groups * k_lhs], refs[groups * k_lhs : groups * k_lhs + k_rhs]
        keep, send = refs[-2:]
        b = jnp.concatenate([r[...] for r in r_refs], 0) if k_rhs > 1 else r_refs[0][...]
        i = pl.program_id(0)
        for g in range(groups):
            a = [r[...] for r in l_refs[g * k_lhs : (g + 1) * k_lhs]]
            a = jnp.concatenate(a, 0) if k_lhs > 1 else a[0]
            out = tn(a, b).astype(BF16)
            for j in range(per):
                pos = table[g * (mg // piece) + i * per + j]
                part = out[j * piece : (j + 1) * piece, :]

                @pl.when(pos < half)
                def _():
                    keep[pos] = part

                @pl.when(pos >= half)
                def _():
                    send[pos - half] = part

    flat = [a for group in lhs for a in group]
    out = sds((half, piece, n), BF16)
    return call(
        body,
        [table, *flat, *rhs],
        [out, out],
        grid=(steps,),
        in_specs=[pl.BlockSpec((a.shape[0], tile), lambda i, *_: (0, i)) for a in flat] + [None] * k_rhs,
        prefetch=1,
        flops=2 * m * n * sum(r.shape[0] for r in rhs),
        name=name,
    )


def flip_dp(x, bit, size):
    return lax.ppermute(x, "dp", [(i, i ^ (1 << bit)) for i in range(size)])


def add_pair(a, b):
    return (a.astype(F32) + b.astype(F32)).astype(BF16)


def sum_pieces(keep, send, size, order):
    got = flip_dp(send, order[0], size)
    for bit in order[1:]:
        half = keep.shape[0] // 2
        keep, send = add_pair(keep[:half], got[:half]), add_pair(keep[half:], got[half:])
        got = flip_dp(send, bit, size)
    whole = add_pair(keep, got)
    for bit in reversed(order[1:]):
        whole = jnp.concatenate([whole, flip_dp(whole, bit, size)], 0)
    return whole, flip_dp(whole, order[0], size)


def place_pieces(inverse, own, other, widths, name):
    half, piece, n = own.shape
    size = 2 * half

    def body(inverse, own_r, other_r, *outs):
        r = pl.program_id(0)

        def put(src):
            at = 0
            for o, width in zip(outs, widths):
                o[...] = src[0, :, at : at + width].astype(F32)
                at += width

        @pl.when(r < half)
        def _():
            put(own_r)

        @pl.when(r >= half)
        def _():
            put(other_r)

    return call(
        body,
        [inverse, own, other],
        [sds((size * piece, width), F32) for width in widths],
        grid=(size,),
        in_specs=[
            pl.BlockSpec((1, piece, n), lambda r, inv: (jnp.minimum(r, half - 1), 0, 0)),
            pl.BlockSpec((1, piece, n), lambda r, inv: (jnp.maximum(r - half, 0), 0, 0)),
        ],
        out_specs=[pl.BlockSpec((piece, width), lambda r, inv: (inv[r], 0)) for width in widths],
        prefetch=1,
        name=name,
    )


def local(
    head_size,
    dp_size,
    tokens,
    out_grad,
    init_state,
    state_grad,
    seq_blocks,
    bucket_table,
    gain_tok,
    gain_state,
    gain_mlp,
    query_tok,
    query_state,
    key_weight,
    value_weight,
    out_tok,
    out_state,
    mlp_in,
    mlp_out,
    gate_forget,
    gate_input,
    rel_bias,
):
    paired = head_size == 2
    chunks = 2 if paired else 1
    rows = tokens.shape[2]
    width = query_tok.shape[1]
    heads = width // HEAD_DIM

    def exchange(x):
        return lax.ppermute(x, "head", [(0, 1), (1, 0)])

    def gather(x):
        return (x, exchange(x)) if paired else (lax.all_gather(x, "head", axis=0, tiled=True),)

    def scatter(parts):
        if paired:
            return (parts[0], exchange(parts[1]))
        return (lax.psum_scatter(parts[0], "head", scatter_dimension=0, tiled=True),)

    first_len = seq_blocks[0, 0]
    live1 = (seq_blocks[0, 0] + seq_blocks[0, 1] > 1).astype(jnp.int32)
    start1 = (first_len == 1).astype(jnp.int32)
    flip = lax.axis_index("head") * rows if paired else jnp.int32(0)
    flags = jnp.stack([live1, start1, flip.astype(jnp.int32), 1 - start1])
    is_live, is_start = live1 > 0, start1 > 0

    onehot = (bucket_table[:, None] == jnp.arange(BUCKETS, dtype=jnp.int32)[None, :]).astype(F32)
    by_dist = jnp.dot(rel_bias.T, onehot.T, precision=lax.Precision.HIGHEST)[:, None, :]

    tok = [tokens[0, 0], tokens[0, 1]]
    init = [init_state[0, 0], init_state[0, 1]]
    cot = [out_grad[0, 0], out_grad[0, 1]]
    scot = [state_grad[0, 0], state_grad[0, 1]]
    live_cot = [cot[0], jnp.where(is_live, cot[1], jnp.zeros_like(cot[1]))]

    tok0_all, st0_all, tok1_all = gather(tok[0]), gather(init[0]), gather(tok[1])
    nt0, qt0, kt0, vt0 = project(tok0_all, gain_tok, query_tok, key_weight, value_weight, "proj_tok0")
    ns0, qs0, ks0, vs0 = project(st0_all, gain_state, query_state, key_weight, value_weight, "proj_state0")
    so0, sc0, pss0, psc0, *sparts = attend_states(qs0, ks0, vs0, kt0, vt0, out_state, chunks, "att_state0")
    sadds0 = scatter(sparts)
    upd0, carried0, state1, sn1 = state_step(
        flags, init[0], init[1], sadds0, gate_forget, gate_input, gain_state, "state_step0"
    )
    sn1_all = gather(sn1)
    to0, tc0, pts0, ptc0, *tparts = attend_tokens(
        flags, qt0, kt0, vt0, None, ks0, vs0, by_dist, out_tok, chunks, "att_tok0"
    )
    tadds0 = scatter(tparts)
    nt1, qt1, kt1, vt1 = project(tok1_all, gain_tok, query_tok, key_weight, value_weight, "proj_tok1")
    mid0, nm0 = mid_norm(tok[0], tadds0, gain_mlp, "mid0")
    nm0_all = gather(nm0)
    cot0_all, cot1_all = gather(live_cot[0]), gather(live_cot[1])
    admit = jax.nn.sigmoid(gate_input)
    snc1 = jnp.where(is_start, scot[1], scot[0]).astype(F32) * live1.astype(F32)
    ug1_all = gather((admit * snc1).astype(BF16))
    ns1, qs1, ks1, vs1 = project(sn1_all, None, query_state, key_weight, value_weight, "proj_state1")
    to1, tc1, pts1, ptc1, *tparts = attend_tokens(
        flags, qt1, kt1, vt1, (kt0, vt0), ks1, vs1, by_dist, out_tok, chunks, "att_tok1"
    )
    tadds1 = scatter(tparts)
    so1, sc1, pss1, psc1, *sparts = attend_states(qs1, ks1, vs1, kt1, vt1, out_state, chunks, "att_state1")
    sadds1 = scatter(sparts)
    mid1, nm1 = mid_norm(tok[1], tadds1, gain_mlp, "mid1")
    nm1_all = gather(nm1)
    hid0, pre0, *mparts = feed_forward(nm0_all, cot0_all, mlp_in, mlp_out, "ff0")
    gadds0 = scatter(mparts[chunks:])
    madds0 = scatter(mparts[:chunks])
    hid1, pre1, *mparts = feed_forward(nm1_all, cot1_all, mlp_in, mlp_out, "ff1")
    gadds1 = scatter(mparts[chunks:])
    madds1 = scatter(mparts[:chunks])

    add_all = lambda adds: functools.reduce(jnp.add, [a.astype(F32) for a in adds])
    new0 = (mid0 + add_all(madds0)).astype(BF16)
    new1 = jnp.where(is_live, (mid1 + add_all(madds1)).astype(BF16), tok[1])
    upd1 = add_all(sadds1)
    forget = jax.nn.sigmoid(gate_forget)
    carried1 = jnp.where(is_live, forget * state1 + admit * upd1, state1)
    next0 = jnp.where(is_start, carried0, carried1)
    next1 = jnp.where(is_start & is_live, carried1, init[1].astype(F32))

    order_a = tuple(range(dp_size.bit_length() - 1))
    index = lax.axis_index("dp")
    table = piece_positions(index, dp_size, order_a)
    inverse = jnp.argsort(table).astype(jnp.int32)
    g_in = weight_grad(table, [[*nm0_all, *nm1_all]], [pre0, pre1], dp_size, "wg_in")
    g_out = weight_grad(table, [[hid0, hid1]], [*cot0_all, *cot1_all], dp_size, "wg_out")

    mg1, mg16, gm1 = mid_back(mid1, gain_mlp, live_cot[1], gadds1, "mid_back1")
    mg1_all = gather(mg16)
    mg0, mg16, gm0 = mid_back(mid0, gain_mlp, live_cot[0], gadds0, "mid_back0")
    mg0_all = gather(mg16)

    dqs1, dkt1, dvt1, dks1, dvs1 = attend_states_back(
        qs1, ks1, vs1, kt1, vt1, pss1, psc1, ug1_all, out_state, [None] * 4, (F32, F32), "att_state_back1"
    )
    dqt1, dkt1, dvt1, dks1, dvs1, bd1, dkp, dvp = attend_tokens_back(
        flags, qt1, kt1, vt1, (kt0, vt0), ks1, vs1, pts1, ptc1, mg1_all, out_tok,
        [dkt1, dvt1, dks1, dvs1], (BF16, BF16), "att_tok_back1",
    )
    sparts = project_back(dqs1, dks1, dvs1, query_state, key_weight, value_weight, chunks, "pb_state1")
    sadds = scatter(sparts)
    ig1, snc0, ug0, gs1, gf1, gi1 = state_back_second(
        flags, state1, gain_state, scot[0], scot[1], upd1, gate_forget, gate_input, sadds, "state_back1"
    )
    ug0_all = gather(ug0)
    tparts = project_back(dqt1, dkt1, dvt1, query_tok, key_weight, value_weight, chunks, "pb_tok1")
    tadds = scatter(tparts)
    row1, gt1 = token_back(flags, LIVE, tok[1], gain_tok, mg1, cot[1], tadds, "tok_back1")
    dqt0, dkt0, dvt0, dks0, dvs0, bd0 = attend_tokens_back(
        flags, qt0, kt0, vt0, None, ks0, vs0, pts0, ptc0, mg0_all, out_tok,
        [dkp, dvp, None, None], (F32, F32), "att_tok_back0",
    )
    g_ot = weight_grad(table, [[to0, to1], [tc0, tc1]], [*mg0_all, *mg1_all], dp_size, "wg_ot")
    dqs0, dkt0, dvt0, dks0, dvs0 = attend_states_back(
        qs0, ks0, vs0, kt0, vt0, pss0, psc0, ug0_all, out_state, [dkt0, dvt0, dks0, dvs0], (BF16, BF16), "att_state_back0"
    )
    g_os = weight_grad(table, [[so0, so1], [sc0, sc1]], [*ug0_all, *ug1_all], dp_size, "wg_os")
    sparts = project_back(dqs0, dks0, dvs0, query_state, key_weight, value_weight, chunks, "pb_state0")
    sadds = scatter(sparts)
    tparts = project_back(dqt0, dkt0, dvt0, query_tok, key_weight, value_weight, chunks, "pb_tok0")
    tadds = scatter(tparts)
    ig0, gs0, gf0, gi0 = state_back_first(
        init[0], gain_state, snc0, upd0, gate_forget, gate_input, sadds, "state_back0"
    )
    row0, gt0 = token_back(flags, None, tok[0], gain_tok, mg0, cot[0], tadds, "tok_back0")
    g_qt = weight_grad(table, [[nt0, nt1]], [dqt0, dqt1], dp_size, "wg_qt")
    g_k = weight_grad(table, [[nt0, nt1, ns0, ns1]], [dkt0, dkt1, dks0, dks1], dp_size, "wg_k")
    g_v = weight_grad(table, [[nt0, nt1, ns0, ns1]], [dvt0, dvt1, dvs0, dvs1], dp_size, "wg_v")
    g_qs = weight_grad(table, [[ns0, ns1]], [dqs0, dqs1], dp_size, "wg_qs")

    def finish(pair, name):
        own, other = sum_pieces(*pair, dp_size, order_a)
        return place_pieces(inverse, own, other, [own.shape[2]], name)[0]

    d_in, d_out = finish(g_in, "pl_in"), finish(g_out, "pl_out")
    d_ot, d_os = finish(g_ot, "pl_ot"), finish(g_os, "pl_os")
    d_qt, d_k, d_v, d_qs = finish(g_qt, "pl_qt"), finish(g_k, "pl_k"), finish(g_v, "pl_v"), finish(g_qs, "pl_qs")

    rel = jnp.dot((bd0 + bd1)[:, 0, :], onehot, precision=lax.Precision.HIGHEST)
    small = jnp.concatenate([gt0 + gt1, gs0 + gs1, gm0 + gm1, gf0 + gf1, gi0 + gi1], 0)
    small = small + exchange(small) if paired else lax.psum(small, "head")
    d = small.shape[1]
    rel_row = jnp.pad(rel.reshape(1, -1), ((0, 0), (0, d - heads * BUCKETS)))
    small = jnp.concatenate([small, rel_row, jnp.zeros((2, d), F32)], 0)
    for bit in order_a:
        small = small + flip_dp(small, bit, dp_size)
    d_rel = small[5, : heads * BUCKETS].reshape(heads, BUCKETS).T

    return (
        jnp.stack([new0, new1])[None],
        jnp.stack([next0, next1])[None],
        jnp.stack([row0, row1])[None],
        jnp.stack([ig0, ig1])[None],
        small[0],
        small[1],
        small[2],
        d_qt,
        d_qs,
        d_k,
        d_v,
        d_ot.reshape(out_tok.shape),
        d_os.reshape(out_state.shape),
        d_in,
        d_out,
        small[3],
        small[4],
        d_rel,
    )


def solution(mesh):
    rows = P("dp", None, "head", None)
    cols = P(None, "head")
    placed = (
        rows, rows, rows, rows, P("dp", None), P(), P(), P(), P(),
        cols, cols, cols, cols, P(None, "head", None), P(None, "head", None), cols, P("head", None),
        P(), P(), cols,
    )
    return jax.shard_map(
        functools.partial(local, mesh.shape["head"], mesh.shape["dp"]),
        mesh=mesh,
        in_specs=placed,
        out_specs=(
            rows, rows, rows, rows, P(), P(), P(),
            cols, cols, cols, cols, P(None, "head", None), P(None, "head", None), cols, P("head", None),
            P(), P(), cols,
        ),
        check_vma=False,
    )
```

```python
import functools
import math

import jax
import jax.numpy as jnp
from jax import lax
from jax.experimental import pallas as pl
from jax.experimental.pallas import tpu as pltpu
from jax.sharding import PartitionSpec as P

HEAD_DIM = 128
WINDOW = 512
BUCKETS = 32
EPSILON = 1e-05
MASKED = -1e30
SCALE = HEAD_DIM ** (-0.5)
F32 = jnp.float32
BF16 = jnp.bfloat16
MIB = 1024 * 1024
COVER = 10**10
LIVE, START, FLIP, PREV = 0, 1, 2, 3
GAIN_TOK, GAIN_STATE, GAIN_MLP, FORGET, ADMIT = 0, 1, 2, 3, 4


def nn(a, b):
    return lax.dot_general(a, b, (((1,), (0,)), ((), ())), preferred_element_type=F32)


def nt(a, b):
    return lax.dot_general(a, b, (((1,), (1,)), ((), ())), preferred_element_type=F32)


def tn(a, b):
    return lax.dot_general(a, b, (((0,), (0,)), ((), ())), preferred_element_type=F32)


def call(body, args, outs, grid=None, in_specs=None, out_specs=None, scratch=(), scalars=0, name=None, vmem=8, cost=COVER):
    smem, whole = pl.BlockSpec(memory_space=pltpu.SMEM), pl.BlockSpec(memory_space=pltpu.VMEM)
    arrays = list(args[scalars:])
    in_specs = list(in_specs or [None] * len(arrays))
    out_specs = list(out_specs or [None] * len(outs))
    outs = list(outs)
    if Order.last is not None:
        arrays[0] = after(arrays[0], Order.last, *Order.arrived)
        Order.arrived = ()
    for k, spec in enumerate(in_specs):
        if spec is not None:
            arrays[k] = pltpu.with_memory_space_constraint(arrays[k], pltpu.HBM)
    for k, spec in enumerate(out_specs):
        if spec is not None:
            outs[k] = pltpu.HBM(outs[k].shape, outs[k].dtype)
    pick = lambda spec: whole if spec is None else pl.BlockSpec(memory_space=pltpu.HBM) if isinstance(spec, str) else spec
    results = pl.pallas_call(
        body,
        out_shape=outs,
        in_specs=[smem] * scalars + [pick(spec) for spec in in_specs],
        out_specs=[pick(spec) for spec in out_specs],
        scratch_shapes=list(scratch),
        compiler_params=pltpu.CompilerParams(vmem_limit_bytes=vmem * MIB),
        cost_estimate=pl.CostEstimate(flops=cost, transcendentals=0, bytes_accessed=0),
        name=name,
        **({"grid": grid} if grid else {}),
    )(*args[:scalars], *arrays)
    Order.last = results[0]
    return results


def after(x, *deps):
    return lax.optimization_barrier((x, *deps))[0]


class Order:
    last = None
    arrived = ()


def arrive(*chunk_lists):
    Order.arrived = (*Order.arrived, *(c[-1] for c in chunk_lists))


def sds(shape, dtype):
    return jax.ShapeDtypeStruct(shape, dtype)


def norm_parts(v):
    mean = jnp.mean(v, axis=-1, keepdims=True)
    cent = v - mean
    var = jnp.mean(cent * cent, axis=-1, keepdims=True)
    inv = lax.rsqrt(var + EPSILON)
    return cent * inv, inv


def norm_back(n, inv, w, g):
    wg = w * g
    return (wg - jnp.mean(wg, -1, keepdims=True) - n * jnp.mean(wg * n, -1, keepdims=True)) * inv


def sum_refs(refs):
    total = refs[0][...].astype(F32)
    for r in refs[1:]:
        total = total + r[...].astype(F32)
    return total


def fetch(pairs, sems):
    copies = [pltpu.make_async_copy(src, dst, sems.at[k]) for k, (src, dst) in enumerate(pairs)]
    for c in copies:
        c.start()
    return copies


def project(chunks, params, gain_at, wq, wk, wv, name):
    count = len(chunks)
    rows, d = chunks[0].shape
    w = wq.shape[1]
    total = rows * count

    def body(*refs):
        xs, p_r, weights, (n_ref, *outs) = refs[:count], refs[count], refs[count + 1 : count + 4], refs[count + 4 : count + 8]
        bufs, sems = refs[count + 8 : count + 11], refs[count + 11]
        copies = fetch(zip(weights, bufs), sems)
        for c in range(count):
            n = xs[c][...]
            if gain_at is not None:
                n = (norm_parts(n.astype(F32))[0] * p_r[gain_at : gain_at + 1, :]).astype(BF16)
            n_ref[c * rows : (c + 1) * rows, :] = n
        for out, buf, copy in zip(outs, bufs, copies):
            copy.wait()
            out[...] = nn(n_ref[...], buf[...]).astype(BF16)

    out = sds((total, w), BF16)
    return call(
        body,
        [*chunks, params, wq, wk, wv],
        [sds((total, d), BF16), out, out, out],
        in_specs=[None] * (count + 1) + ["hbm"] * 3,
        scratch=[pltpu.VMEM((d, w), BF16)] * 3 + [pltpu.SemaphoreType.DMA((3,))],
        name=name,
        vmem=10,
    )


def lanes(h):
    return pl.ds(pl.multiple_of(h * HEAD_DIM, HEAD_DIM), HEAD_DIM)


def softmax_cols(s):
    e = jnp.exp(s - jnp.max(s, axis=0, keepdims=True))
    return (e * (1.0 / jnp.sum(e, axis=0, keepdims=True))).astype(BF16)


def write_parts(value, parts, rows):
    for c, part in enumerate(parts):
        part[...] = value[c * rows : (c + 1) * rows, :].astype(BF16)


def window_masks(flip):
    key_row = lax.broadcasted_iota(jnp.int32, (WINDOW, WINDOW), 0) ^ flip
    query_row = lax.broadcasted_iota(jnp.int32, (WINDOW, WINDOW), 1) ^ flip
    return key_row, query_row


def out_copies(buf, outs, sems, h, slot):
    return [pltpu.make_async_copy(buf.at[slot, k], o.at[h], sems.at[slot, k]) for k, o in enumerate(outs)]


def attend(flags, q, selfs, cross, by_dist, prev, ow, chunks, name):
    t, w = q.shape
    d = ow.shape[2]
    heads = w // HEAD_DIM
    rows = t // chunks
    window = by_dist is not None
    arrays = [q, *selfs, *cross] + ([by_dist] if window else []) + (list(prev) if prev else []) + [ow]

    def body(flags, *refs):
        refs = list(refs)
        q_r, ka_r, va_r, kb_r, vb_r = refs[:5]
        del refs[:5]
        if window:
            f_r = refs.pop(0)
        if prev:
            kp_r, vp_r = refs.pop(0), refs.pop(0)
        ow_r, out_r, pa_o, pb_o = refs[:4]
        parts, (pbuf, sems, obuf, osem) = refs[4:-4], refs[-4:]
        (ow_copy,) = fetch([(ow_r, obuf)], osem)
        flip, prev_ok = flags[FLIP], flags[PREV]

        def step(h, carry):
            slot = h % 2
            at = lanes(h)

            @pl.when(h >= 2)
            def _():
                for c in out_copies(pbuf, (pa_o, pb_o), sems, h - 2, slot):
                    c.wait()

            qv = q_r[:, at]
            s = nt(ka_r[:, at], qv)
            if window:
                key_row, query_row = window_masks(flip)
                tri = allowed = key_row <= query_row
                if prev:
                    s = jnp.where(tri, s, nt(kp_r[:, at], qv))
                    allowed = key_row <= query_row + prev_ok * (2 * WINDOW)
                bias = pltpu.roll(jnp.broadcast_to(f_r[h], (WINDOW, WINDOW)), 0, 1, stride=1, stride_axis=0)
                s = jnp.where(allowed, s * SCALE + bias, MASKED)
            else:
                s = s * SCALE
            p = softmax_cols(s)
            pbuf[slot, 0] = p
            if prev:
                zero = jnp.zeros_like(p)
                o = tn(jnp.where(tri, p, zero), va_r[:, at]) + tn(jnp.where(tri, zero, p), vp_r[:, at])
            else:
                o = tn(p, va_r[:, at])
            out_r[0, :, at] = o.astype(BF16)
            p = softmax_cols(nt(kb_r[:, at], qv) * SCALE)
            pbuf[slot, 1] = p
            out_r[1, :, at] = tn(p, vb_r[:, at]).astype(BF16)
            for c in out_copies(pbuf, (pa_o, pb_o), sems, h, slot):
                c.start()
            return carry

        lax.fori_loop(0, heads, step, 0)
        ow_copy.wait()
        write_parts(nn(out_r[0], obuf[0]) + nn(out_r[1], obuf[1]), parts, rows)
        for h in range(max(0, heads - 2), heads):
            for c in out_copies(pbuf, (pa_o, pb_o), sems, h, h % 2):
                c.wait()

    probs = sds((heads, WINDOW, t), BF16)
    return call(
        body,
        [flags, *arrays],
        [sds((2, t, w), BF16), probs, probs] + [sds((rows, d), BF16)] * chunks,
        in_specs=[None] * (len(arrays) - 1) + ["hbm"],
        out_specs=[None, "hbm", "hbm"] + [None] * chunks,
        scratch=[
            pltpu.VMEM((2, 2, WINDOW, t), BF16),
            pltpu.SemaphoreType.DMA((2, 2)),
            pltpu.VMEM((2, w, d), BF16),
            pltpu.SemaphoreType.DMA((1,)),
        ],
        scalars=1,
        name=name,
        vmem=14,
    )


def score_back(p16, dp):
    p = p16.astype(F32)
    t = p * dp
    return (t - p * jnp.sum(t, axis=0, keepdims=True)).astype(BF16)


def distance_sums(ds):
    x = ds.astype(F32)
    n = WINDOW
    while n > 1:
        n //= 2
        x = x[:n] + pltpu.roll(x[n:], WINDOW - n, 1)
    return x


def attend_back(flags, q, selfs, cross, window, prev, pa, pb, branch, ow, adds, final, name):
    t, w = q.shape
    d = ow.shape[2]
    heads = w // HEAD_DIM
    count = len(branch)
    rows = t // count
    given = [a for a in adds if a is not None]
    arrays = [q, *selfs, *cross] + (list(prev) if prev else []) + [pa, pb, *branch, ow, *given]
    n_first = 7 if prev else 5

    def body(flags, *refs):
        refs = list(refs)
        q_r, ka_r, va_r, kb_r, vb_r = refs[:5]
        del refs[:5]
        if prev:
            kp_r, vp_r = refs.pop(0), refs.pop(0)
        pa_i, pb_i = refs.pop(0), refs.pop(0)
        br = refs[:count]
        ow_r = refs[count]
        del refs[: count + 1]
        add_refs = [None if a is None else refs.pop(0) for a in adds]
        dq_r, dka_r, dva_r, dkb_r, dvb_r = refs[:5]
        del refs[:5]
        if window:
            bd_r = refs.pop(0)
        if prev:
            dkp_r, dvp_r = refs.pop(0), refs.pop(0)
        do_r, pbuf, sems, obuf, osem = refs
        (ow_copy,) = fetch([(ow_r, obuf)], osem)
        flip = flags[FLIP]

        def loads(h, slot):
            return [pltpu.make_async_copy(p.at[h], pbuf.at[slot, k], sems.at[slot, k]) for k, p in enumerate((pa_i, pb_i))]

        for c in loads(0, 0):
            c.start()
        ow_copy.wait()
        for c in range(count):
            for k in range(2):
                do_r[k, c * rows : (c + 1) * rows, :] = nt(br[c][...], obuf[k]).astype(BF16)

        def step(h, carry):
            slot = h % 2
            at = lanes(h)

            @pl.when(h + 1 < heads)
            def _():
                for c in loads(h + 1, 1 - slot):
                    c.start()

            for c in loads(h, slot):
                c.wait()

            def put(ref, value, add):
                if add is not None:
                    value = value + add[:, at].astype(F32)
                ref[:, at] = value.astype(ref.dtype)

            qv, do_a, do_b = q_r[:, at], do_r[0, :, at], do_r[1, :, at]
            p16 = pbuf[slot, 0]
            dp = nt(va_r[:, at], do_a)
            if prev:
                key_row, query_row = window_masks(flip)
                tri = key_row <= query_row
                dp = jnp.where(tri, dp, nt(vp_r[:, at], do_a))
            ds = score_back(p16, dp)
            if window:
                bd_r[h] = distance_sums(ds)
            if prev:
                zero = jnp.zeros_like(ds)
                p_prev, ds_prev = jnp.where(tri, zero, p16), jnp.where(tri, zero, ds)
                p16, ds = jnp.where(tri, p16, zero), jnp.where(tri, ds, zero)
                dvp_r[:, at] = nn(p_prev, do_a)
                dkp_r[:, at] = nn(ds_prev, qv) * SCALE
            put(dva_r, nn(p16, do_a), add_refs[1])
            put(dka_r, nn(ds, qv) * SCALE, add_refs[0])
            dq = tn(ds, ka_r[:, at])
            if prev:
                dq = dq + tn(ds_prev, kp_r[:, at])
            p16 = pbuf[slot, 1]
            ds = score_back(p16, nt(vb_r[:, at], do_b))
            put(dvb_r, nn(p16, do_b), add_refs[3])
            put(dkb_r, nn(ds, qv) * SCALE, add_refs[2])
            dq = dq + tn(ds, kb_r[:, at])
            dq_r[:, at] = (dq * SCALE).astype(BF16)
            return carry

        lax.fori_loop(0, heads, step, 0)

    full = lambda dt: sds((t, w), dt)
    outs = [full(BF16), full(final[0]), full(final[0]), full(final[1]), full(final[1])]
    if window:
        outs.append(sds((heads, 1, WINDOW), F32))
    if prev:
        outs += [full(F32)] * 2
    return call(
        body,
        [flags, *arrays],
        outs,
        in_specs=[None] * n_first + ["hbm"] * 2 + [None] * count + ["hbm"] + [None] * len(given),
        scratch=[
            pltpu.VMEM((2, t, w), BF16),
            pltpu.VMEM((2, 2, WINDOW, t), BF16),
            pltpu.SemaphoreType.DMA((2, 2)),
            pltpu.VMEM((2, w, d), BF16),
            pltpu.SemaphoreType.DMA((1,)),
        ],
        scalars=1,
        name=name,
        vmem=14,
    )


def project_back(dq, dk, dv, wq, wk, wv, chunks, name):
    t, w = dq.shape
    d = wq.shape[0]
    rows = t // chunks

    def body(*refs):
        grads, weights, parts, bufs, sems = refs[:3], refs[3:6], refs[6:-4], refs[-4:-1], refs[-1]
        copies = fetch(zip(weights, bufs), sems)
        for c in copies:
            c.wait()
        for c, part in enumerate(parts):
            at = slice(c * rows, (c + 1) * rows)
            total = nt(grads[0][at, :], bufs[0][...])
            for g, buf in zip(grads[1:], bufs[1:]):
                total = total + nt(g[at, :], buf[...])
            part[...] = total.astype(BF16)

    return call(
        body,
        [dq, dk, dv, wq, wk, wv],
        [sds((rows, d), BF16)] * chunks,
        in_specs=[None] * 3 + ["hbm"] * 3,
        scratch=[pltpu.VMEM((d, w), BF16)] * 3 + [pltpu.SemaphoreType.DMA((3,))],
        name=name,
        vmem=10,
    )


def feed_forward(normed, cots, w_in, w_out, name):
    count = len(normed)
    rows, d = normed[0].shape
    f = w_in.shape[1]
    tile = min(f, 512)
    t = rows * count
    c0 = math.sqrt(2.0 / math.pi)

    def body(*refs):
        nm, og = refs[:count], refs[count : 2 * count]
        wi_r, wo_r, hid_r, pre_r = refs[2 * count : 2 * count + 4]
        rest = refs[2 * count + 4 :]
        parts_y, parts_g, (acc_y, acc_g, ibuf, obuf, sems) = rest[:count], rest[count : 2 * count], rest[-5:]

        def loads(i, slot):
            cols = pl.ds(pl.multiple_of(i * tile, tile), tile)
            return [
                pltpu.make_async_copy(wi_r.at[:, cols], ibuf.at[slot], sems.at[slot, 0]),
                pltpu.make_async_copy(wo_r.at[cols, :], obuf.at[slot], sems.at[slot, 1]),
            ]

        for c in loads(0, 0):
            c.start()
        acc_y[...] = jnp.zeros_like(acc_y)
        acc_g[...] = jnp.zeros_like(acc_g)

        def step(i, carry):
            cols = pl.ds(pl.multiple_of(i * tile, tile), tile)
            slot = i % 2

            @pl.when(i + 1 < f // tile)
            def _():
                for c in loads(i + 1, 1 - slot):
                    c.start()

            for c in loads(i, slot):
                c.wait()
            wi, wo = ibuf[slot], obuf[slot]
            for c in range(count):
                at = slice(c * rows, (c + 1) * rows)
                v = nn(nm[c][...], wi)
                sq = v * v
                th = jnp.tanh(v * (c0 + c0 * 0.044715 * sq))
                half = 0.5 + 0.5 * th
                hidden = (v * half).astype(BF16)
                slope = half + (0.5 * v) * (1.0 - th * th) * (c0 + 3.0 * c0 * 0.044715 * sq)
                hid_r[at, cols] = hidden
                pre = (nt(og[c][...], wo) * slope).astype(BF16)
                pre_r[at, cols] = pre
                acc_y[at, :] += nn(hidden, wo)
                acc_g[at, :] += nt(pre, wi)
            return carry

        lax.fori_loop(0, f // tile, step, 0)
        write_parts(acc_y, parts_y, rows)
        write_parts(acc_g, parts_g, rows)

    return call(
        body,
        [*normed, *cots, w_in, w_out],
        [sds((t, f), BF16)] * 2 + [sds((rows, d), BF16)] * (2 * count),
        in_specs=[None] * (2 * count) + ["hbm"] * 2,
        scratch=[pltpu.VMEM((t, d), F32)] * 2
        + [pltpu.VMEM((2, d, tile), BF16), pltpu.VMEM((2, tile, d), BF16), pltpu.SemaphoreType.DMA((2, 2))],
        name=name,
        vmem=18,
    )


def row_call(body, flags, arrays, outs, name, cost=0):
    n_in = len(arrays)

    def wrapped(flags, *refs):
        values = body(flags, *refs[:n_in])
        for o, v in zip(refs[n_in:], values):
            o[...] = jnp.sum(v, 0, keepdims=True) if o.shape[0] == 1 else v.astype(o.dtype)

    return call(wrapped, [flags, *arrays], outs, scalars=1, name=name, cost=cost)


def f32(ref):
    return ref[...].astype(F32)


def param(p_r, at):
    return p_r[at : at + 1, :]


def mid_norm(flags, tok, adds, params, name):
    def body(flags, tok_r, p_r, *adds_r):
        mid = f32(tok_r) + sum_refs(adds_r)
        return mid, norm_parts(mid)[0] * param(p_r, GAIN_MLP)

    return row_call(body, flags, [tok, params, *adds], [sds(tok.shape, F32), sds(tok.shape, BF16)], name)


def state_step(flags, first, second, adds, params, name):
    def body(flags, a_r, b_r, p_r, *adds_r):
        upd = sum_refs(adds_r)
        car = param(p_r, FORGET) * f32(a_r) + param(p_r, ADMIT) * upd
        st = jnp.where(flags[START].astype(F32) > 0.5, f32(b_r), car)
        return upd, car, st, norm_parts(st)[0] * param(p_r, GAIN_STATE)

    full = sds(first.shape, F32)
    arrays = [first, second, params, *adds]
    return row_call(body, flags, arrays, [full, full, full, sds(first.shape, BF16)], name)


def mid_back(flags, mid, params, cot, adds, name, cost=0):
    def body(flags, mid_r, p_r, cot_r, *adds_r):
        n, inv = norm_parts(mid_r[...])
        g = sum_refs(adds_r)
        mg = f32(cot_r) + norm_back(n, inv, param(p_r, GAIN_MLP), g)
        return mg, mg, g * n

    outs = [sds(mid.shape, F32), sds(mid.shape, BF16), sds((1, mid.shape[1]), F32)]
    return row_call(body, flags, [mid, params, cot, *adds], outs, name, cost)


def token_back(flags, live_at, tok, params, mg, cot, adds, name):
    def body(flags, tok_r, p_r, mg_r, cot_r, *adds_r):
        n, inv = norm_parts(f32(tok_r))
        g = sum_refs(adds_r)
        row = mg_r[...] + norm_back(n, inv, param(p_r, GAIN_TOK), g)
        if live_at is not None:
            row = jnp.where(flags[live_at].astype(F32) > 0.5, row, f32(cot_r))
        return row, g * n

    outs = [sds(tok.shape, F32), sds((1, tok.shape[1]), F32)]
    return row_call(body, flags, [tok, params, mg, cot, *adds], outs, name)


def gate_terms(snc, upd, state, p_r):
    sf, si = param(p_r, FORGET), param(p_r, ADMIT)
    return sf, si, snc * state * (sf * (1.0 - sf)), snc * upd * (si * (1.0 - si))


def state_back_second(flags, state, params, cot0, cot1, upd, adds, name):
    n_upd = len(upd)

    def body(flags, st_r, p_r, c0_r, c1_r, *rest):
        upd_v, adds_r = sum_refs(rest[:n_upd]), rest[n_upd:]
        live = flags[LIVE].astype(F32)
        start = flags[START].astype(F32)
        c0, c1 = f32(c0_r), f32(c1_r)
        snc = jnp.where(start > 0.5, c1, c0) * live
        st = st_r[...]
        n, inv = norm_parts(st)
        g = sum_refs(adds_r)
        sf, si, gf, gi = gate_terms(snc, upd_v, st, p_r)
        back = jnp.where(live > 0.5, sf * snc + norm_back(n, inv, param(p_r, GAIN_STATE), g), snc)
        snc0 = jnp.where(start > 0.5, c0, back)
        return jnp.where(start * live > 0.5, back, c1), snc0, si * snc0, g * n, gf, gi

    full, row = sds(state.shape, F32), sds((1, state.shape[1]), F32)
    arrays = [state, params, cot0, cot1, *upd, *adds]
    return row_call(body, flags, arrays, [full, full, sds(state.shape, BF16), row, row, row], name)


def state_back_first(flags, state, params, snc, upd, adds, name):
    def body(flags, st_r, p_r, snc_r, upd_r, *adds_r):
        st = f32(st_r)
        n, inv = norm_parts(st)
        g = sum_refs(adds_r)
        snc = snc_r[...]
        sf, _, gf, gi = gate_terms(snc, upd_r[...], st, p_r)
        return sf * snc + norm_back(n, inv, param(p_r, GAIN_STATE), g), g * n, gf, gi

    full, row = sds(state.shape, F32), sds((1, state.shape[1]), F32)
    arrays = [state, params, snc, upd, *adds]
    return row_call(body, flags, arrays, [full, row, row, row], name)


def piece_positions(index, size, order):
    rel = jnp.arange(size, dtype=jnp.int32) ^ index
    pos = jnp.zeros((size,), jnp.int32)
    for bit in order:
        pos = pos * 2 + ((rel >> bit) & 1)
    return pos


def weight_grads(table, jobs, size, name, cost=COVER):
    width = lambda a: a.shape[-1] * (2 if a.ndim == 3 else 1)
    first = lambda b: b[0] if isinstance(b, tuple) else b
    m = width(jobs[0][0][0])
    assert all(width(a) == m for lhs, _ in jobs for a in lhs)
    cols = [first(rhs[0][0]).shape[1] for _, rhs in jobs]
    n = sum(cols)
    tile = min([256] + [a.shape[-1] for lhs, _ in jobs for a in lhs])
    flat, plan = [], []

    def add(a):
        for k, b in enumerate(flat):
            if b is a:
                return k
        flat.append(a)
        return len(flat) - 1

    for lhs, rhs in jobs:
        parts = []
        for a, group in zip(lhs, rhs):
            at, row = add(a), 0
            for b in group:
                b, start, count = b if isinstance(b, tuple) else (b, 0, b.shape[0])
                parts.append((at, row, count, add(b), start))
                row += count
            assert row == a.shape[-2]
        plan.append(parts)
    shapes = [a.shape for a in flat]
    piece = m // size
    half = size // 2

    def body(*refs):
        table, refs = (None, refs) if len(refs) == len(flat) + 1 else (refs[0], refs[1:])

        def step(i, carry):
            col = 0
            for parts, width in zip(plan, cols):
                total = None
                for at, row, count, other, start in parts:
                    if len(shapes[at]) == 3:
                        blocks = shapes[at][2] // tile
                        here = pl.ds(pl.multiple_of((i % blocks) * tile, tile), tile)
                        a = refs[at][i // blocks, row : row + count, here]
                    else:
                        a = refs[at][row : row + count, pl.ds(pl.multiple_of(i * tile, tile), tile)]
                    term = tn(a, refs[other][start : start + count, :])
                    total = term if total is None else total + term
                out = total.astype(BF16)
                if table is None:
                    refs[-1][pl.ds(pl.multiple_of(i * tile, tile), tile), col : col + width] = out
                else:
                    keep, send = refs[-2:]
                    for j in range(tile // piece):
                        pos = table[i * (tile // piece) + j]
                        part = out[j * piece : (j + 1) * piece, :]

                        @pl.when(pos < half)
                        def _():
                            keep[pos, :, col : col + width] = part

                        @pl.when(pos >= half)
                        def _():
                            send[pos - half, :, col : col + width] = part

                col += width
            return carry

        lax.fori_loop(0, m // tile, step, 0)

    if table is None:
        outs = [sds((m, n), BF16)]
    else:
        outs = [sds((half, piece, n), BF16)] * 2
    args = flat if table is None else [table, *flat]
    return call(body, args, outs, scalars=len(args) - len(flat), name=name, vmem=12, cost=cost), cols


def split_rows(a, count):
    rows = a.shape[0] // count
    return [(a, k * rows, rows) for k in range(count)]


def widen(a, name):
    rows, n = a.shape
    tile = min(rows, 256)
    spec = pl.BlockSpec((tile, n), lambda i: (i, 0))

    def body(a_r, o_r):
        o_r[...] = a_r[...].astype(F32)

    return call(body, [a], [sds(a.shape, F32)], grid=(rows // tile,), in_specs=[spec], out_specs=[spec], name=name)[0]


def flip_dp(x, bit, size):
    return lax.ppermute(x, "dp", [(i, i ^ (1 << bit)) for i in range(size)])


def add_pair(a, b):
    return (a.astype(F32) + b.astype(F32)).astype(BF16)


def in_turn(x):
    return x if Order.last is None else after(x, Order.last)


def sum_pieces(pair, size, order):
    keep, send = pair
    got = flip_dp(send, order[0], size)
    yield
    for bit in order[1:]:
        half = keep.shape[0] // 2
        got = in_turn(got)
        keep, send = add_pair(keep[:half], got[:half]), add_pair(keep[half:], got[half:])
        Order.last = send
        got = flip_dp(send, bit, size)
        yield
    whole = add_pair(keep, in_turn(got))
    for bit in reversed(order[1:]):
        Order.last = whole
        got = flip_dp(whole, bit, size)
        yield
        whole = jnp.concatenate([whole, in_turn(got)], 0)
    Order.last = whole
    got = flip_dp(whole, order[0], size)
    yield
    yield whole, got


def sum_small(x, size, order):
    for bit in order:
        got = flip_dp(x, bit, size)
        yield
        x = x + in_turn(got)
        Order.last = x
    yield x


def place_pieces(table, own, other, widths, name):
    half, piece, n = own.shape
    size = 2 * half
    per = max(1, 256 // piece)

    def body(table, own_r, other_r, *outs):
        for j in range(per):
            pos = table[pl.program_id(0) * per + j]
            rows = slice(j * piece, (j + 1) * piece)

            def put(src, at):
                start = 0
                for o, width in zip(outs, widths):
                    o[rows, :] = src[at, :, start : start + width].astype(F32)
                    start += width

            @pl.when(pos < half)
            def _():
                put(own_r, pos)

            @pl.when(pos >= half)
            def _():
                put(other_r, pos - half)

    return call(
        body,
        [table, own, other],
        [sds((size * piece, width), F32) for width in widths],
        grid=(size // per,),
        in_specs=[pl.BlockSpec(own.shape, lambda i: (0, 0, 0), pipeline_mode=pl.Buffered(1))] * 2,
        out_specs=[pl.BlockSpec((per * piece, width), lambda i: (i, 0)) for width in widths],
        scalars=1,
        name=name,
        vmem=24,
    )


def local(
    head_size,
    dp_size,
    tokens,
    out_grad,
    init_state,
    state_grad,
    seq_blocks,
    bucket_table,
    gain_tok,
    gain_state,
    gain_mlp,
    query_tok,
    query_state,
    key_weight,
    value_weight,
    out_tok,
    out_state,
    mlp_in,
    mlp_out,
    gate_forget,
    gate_input,
    rel_bias,
):
    paired = head_size == 2
    chunks = 2 if paired else 1
    rows = tokens.shape[2]
    width = query_tok.shape[1]
    heads = width // HEAD_DIM

    def exchange(x):
        return lax.ppermute(x, "head", [(0, 1), (1, 0)])

    def gather(x):
        return (x, exchange(x)) if paired else (lax.all_gather(x, "head", axis=0, tiled=True),)

    def scatter(parts):
        if paired:
            return (parts[0], exchange(parts[1]))
        return (lax.psum_scatter(parts[0], "head", scatter_dimension=0, tiled=True),)

    first_len = seq_blocks[0, 0]
    live1 = (seq_blocks[0, 0] + seq_blocks[0, 1] > 1).astype(jnp.int32)
    start1 = (first_len == 1).astype(jnp.int32)
    flip = lax.axis_index("head") * rows if paired else jnp.int32(0)
    flags = jnp.stack([live1, start1, flip.astype(jnp.int32), 1 - start1])
    is_live, is_start = live1 > 0, start1 > 0

    onehot = (bucket_table[:, None] == jnp.arange(BUCKETS, dtype=jnp.int32)[None, :]).astype(F32)
    by_dist = jnp.dot(rel_bias.T, onehot.T, precision=lax.Precision.HIGHEST)[:, None, :]

    tok = [tokens[0, 0], tokens[0, 1]]
    init = [init_state[0, 0], init_state[0, 1]]
    cot = [out_grad[0, 0], out_grad[0, 1]]
    scot = [state_grad[0, 0], state_grad[0, 1]]
    live_cot = [cot[0], jnp.where(is_live, cot[1], jnp.zeros_like(cot[1]))]

    admit, forget = jax.nn.sigmoid(gate_input), jax.nn.sigmoid(gate_forget)
    bits = tuple(range(dp_size.bit_length() - 1))
    orders = (bits, bits[:1] + bits[2:] + bits[1:2])
    tables = [piece_positions(lax.axis_index("dp"), dp_size, order) for order in orders]
    add_all = lambda adds: functools.reduce(jnp.add, [a.astype(F32) for a in adds])
    hold = lambda parts, dep: [*parts[:-1], after(parts[-1], dep)]
    Order.last, Order.arrived = None, ()
    params = jnp.stack([gain_tok, gain_state, gain_mlp, forget, admit])
    params = jnp.concatenate([params, jnp.zeros((3, params.shape[1]), F32)], 0)

    def weight_sum(which, jobs, name):
        rows_of = lambda job: job[0][0].shape[-1] * (2 if job[0][0].ndim == 3 else 1)
        groups = {}
        for k, job in enumerate(jobs):
            groups.setdefault(rows_of(job), []).append(k)
        steps, cols = [], []
        for m, members in groups.items():
            pair, width = weight_grads(tables[which], [jobs[k] for k in members], dp_size, name)
            steps.append(sum_pieces(pair, dp_size, orders[which]))
            next(steps[-1])
            cols.append(width)
        return dict(steps=steps, which=which, cols=cols, members=list(groups.values()), name=name, pieces=None, grads=None)

    def advance(*sums):
        for w in sums:
            brought = [next(steps) for steps in w["steps"]]
            if brought[0] is not None:
                w["pieces"] = brought

    def place(w):
        grads = {}
        for members, pieces, cols in zip(w["members"], w["pieces"], w["cols"]):
            for k, grad in zip(members, place_pieces(tables[w["which"]], *pieces, cols, "pl_" + w["name"])):
                grads[k] = grad
        w["grads"] = [grads[k] for k in sorted(grads)]

    tok0_all, st0_all, tok1_all, cot1_all = gather(tok[0]), gather(init[0]), gather(tok[1]), gather(live_cot[1])
    nt0, qt0, kt0, vt0 = project(tok0_all, params, GAIN_TOK, query_tok, key_weight, value_weight, "proj_tok0")
    ns0, qs0, ks0, vs0 = project(st0_all, params, GAIN_STATE, query_state, key_weight, value_weight, "proj_state0")
    os0, pss0, psc0, *sparts = attend(
        flags, qs0, (ks0, vs0), (kt0, vt0), None, None, out_state, chunks, "att_state0"
    )
    sadds0 = scatter(sparts)
    nt1, qt1, kt1, vt1 = project(tok1_all, params, GAIN_TOK, query_tok, key_weight, value_weight, "proj_tok1")
    upd0, carried0, state1, sn1 = state_step(
        flags, init[0], init[1], sadds0, params, "state_step0"
    )
    sn1_all = gather(sn1)
    cot0_all = gather(after(live_cot[0], sn1))
    ot0, pts0, ptc0, *tparts = attend(
        flags, qt0, (kt0, vt0), (ks0, vs0), by_dist, None, out_tok, chunks, "att_tok0"
    )
    tadds0 = scatter(tparts)
    arrive(cot1_all)
    ns1, qs1, ks1, vs1 = project(sn1_all, params, None, query_state, key_weight, value_weight, "proj_state1")
    ot1, pts1, ptc1, *tparts = attend(
        flags, qt1, (kt1, vt1), (ks1, vs1), by_dist, (kt0, vt0), out_tok, chunks, "att_tok1"
    )
    tadds1 = scatter(tparts)
    mid0, nm0 = mid_norm(flags, tok[0], tadds0, params, "mid0")
    nm0_all = gather(nm0)
    arrive(cot0_all)
    os1, pss1, psc1, *sparts1 = attend(
        flags, qs1, (ks1, vs1), (kt1, vt1), None, None, out_state, chunks, "att_state1"
    )
    mid1, nm1 = mid_norm(flags, tok[1], tadds1, params, "mid1")
    nm1_all = gather(nm1)
    snc1 = jnp.where(is_start, scot[1], scot[0]).astype(F32) * live1.astype(F32)
    hid0, pre0, *mparts0 = feed_forward(nm0_all, cot0_all, mlp_in, mlp_out, "ff0")
    gadds0 = scatter(mparts0[chunks:])
    ug1_all = gather(after((admit * snc1).astype(BF16), hid0))
    hid1, pre1, *mparts1 = feed_forward(nm1_all, cot1_all, mlp_in, mlp_out, "ff1")
    gadds1 = scatter(mparts1[chunks:])

    (g_in,), _ = weight_grads(
        None, [([*nm0_all, *nm1_all], [[p] for p in split_rows(pre0, chunks) + split_rows(pre1, chunks)])], dp_size, "wg_in"
    )
    arrive(ug1_all)
    (g_out,), _ = weight_grads(None, [([hid0, hid1], [cot0_all, cot1_all])], dp_size, "wg_out", 0)
    d_in, d_out = lax.psum((g_in, g_out), "dp")
    mg1, mg16b, gm1 = mid_back(flags, mid1, params, live_cot[1], gadds1, "mid_back1")
    mg1_all = gather(mg16b)
    mg0, mg16, gm0 = mid_back(flags, mid0, params, live_cot[0], gadds0, "mid_back0")
    mg0_all = gather(mg16)
    dqs1, dks1, dvs1, dkt1, dvt1 = attend_back(
        flags, qs1, (ks1, vs1), (kt1, vt1), False, None, pss1, psc1, ug1_all, out_state, [None] * 4, (F32, F32), "att_state_back1"
    )
    sadds1 = scatter(hold(sparts1, dqs1))
    dqt1, dkt1, dvt1, dks1, dvs1, bd1, dkp, dvp = attend_back(
        flags, qt1, (kt1, vt1), (ks1, vs1), True, (kt0, vt0), pts1, ptc1, mg1_all, out_tok,
        [dkt1, dvt1, dks1, dvs1], (BF16, BF16), "att_tok_back1",
    )
    sback1 = project_back(dqs1, dks1, dvs1, query_state, key_weight, value_weight, chunks, "pb_state1")
    sback1 = scatter(sback1)
    dqt0, dkt0, dvt0, dks0, dvs0, bd0 = attend_back(
        flags, qt0, (kt0, vt0), (ks0, vs0), True, None, pts0, ptc0, mg0_all, out_tok,
        [dkp, dvp, None, None], (F32, F32), "att_tok_back0",
    )
    ig1, snc0, ug0, gs1, gf1, gi1 = state_back_second(
        flags, state1, params, scot[0], scot[1], sadds1, sback1, "state_back1"
    )
    ug0_all = gather(ug0)
    w_early = weight_sum(0, [([ot0, ot1], [mg0_all, mg1_all]), ([nt0, nt1], [[dqt0], [dqt1]])], "wg_early")
    madds0 = scatter(hold(mparts0[:chunks], ug0_all[-1]))
    madds1 = scatter(hold(mparts1[:chunks], ug0_all[-1]))
    dqs0, dks0, dvs0, dkt0, dvt0 = attend_back(
        flags, qs0, (ks0, vs0), (kt0, vt0), False, None, pss0, psc0, ug0_all, out_state,
        [dks0, dvs0, dkt0, dvt0], (BF16, BF16), "att_state_back0",
    )
    advance(w_early)
    sback0 = project_back(dqs0, dks0, dvs0, query_state, key_weight, value_weight, chunks, "pb_state0")
    sback0 = scatter(sback0)
    normed_all = [nt0, nt1, ns0, ns1]
    w_kv = weight_sum(
        0, [(normed_all, [[dkt0], [dkt1], [dks0], [dks1]]), (normed_all, [[dvt0], [dvt1], [dvs0], [dvs1]])], "wg_kv"
    )
    w_late = weight_sum(1, [([os0, os1], [ug0_all, ug1_all]), ([ns0, ns1], [[dqs0], [dqs1]])], "wg_late")
    advance(w_early, w_kv)
    arrive(madds0, madds1)
    tback0 = project_back(dqt0, dkt0, dvt0, query_tok, key_weight, value_weight, chunks, "pb_tok0")
    tback0 = scatter(tback0)
    tback1 = project_back(dqt1, dkt1, dvt1, query_tok, key_weight, value_weight, chunks, "pb_tok1")
    tback1 = scatter(tback1)
    advance(w_late)
    ig0, gs0, gf0, gi0 = state_back_first(
        flags, init[0], params, snc0, upd0, sback0, "state_back0"
    )
    row0, gt0 = token_back(flags, None, tok[0], params, mg0, cot[0], tback0, "tok_back0")
    row1, gt1 = token_back(flags, LIVE, tok[1], params, mg1, cot[1], tback1, "tok_back1")

    rel = jnp.dot((bd0 + bd1)[:, 0, :], onehot, precision=lax.Precision.HIGHEST)
    small = jnp.concatenate([gt0 + gt1, gs0 + gs1, gm0 + gm1, gf0 + gf1, gi0 + gi1], 0)
    small = small + exchange(small) if paired else lax.psum(small, "head")
    d = small.shape[1]
    rel_row = jnp.pad(rel.reshape(1, -1), ((0, 0), (0, d - heads * BUCKETS)))
    small = jnp.concatenate([small, rel_row, jnp.zeros((2, d), F32)], 0)
    w_small = dict(steps=[sum_small(small, dp_size, bits)], pieces=None)

    running = [w_early, w_kv, w_late, w_small]
    while running:
        advance(*running)
        for w in list(running):
            if w["pieces"] is not None:
                running.remove(w)
                if w is not w_small:
                    place(w)
    (d_ot, d_qt), (d_k, d_v), (d_os, d_qs) = w_early["grads"], w_kv["grads"], w_late["grads"]
    (small,) = w_small["pieces"]
    d_in, d_out = widen(d_in, "widen_in"), widen(d_out, "widen_out")
    d_rel = small[5, : heads * BUCKETS].reshape(heads, BUCKETS).T

    new0 = (mid0 + add_all(madds0)).astype(BF16)
    new1 = jnp.where(is_live, (mid1 + add_all(madds1)).astype(BF16), tok[1])
    carried1 = jnp.where(is_live, forget * state1 + admit * add_all(sadds1), state1)
    next0 = jnp.where(is_start, carried0, carried1)
    next1 = jnp.where(is_start & is_live, carried1, init[1].astype(F32))

    return (
        jnp.stack([new0, new1])[None],
        jnp.stack([next0, next1])[None],
        jnp.stack([row0, row1])[None],
        jnp.stack([ig0, ig1])[None],
        small[0],
        small[1],
        small[2],
        d_qt,
        d_qs,
        d_k,
        d_v,
        d_ot.reshape(out_tok.shape),
        d_os.reshape(out_state.shape),
        d_in,
        d_out,
        small[3],
        small[4],
        d_rel,
    )


def solution(mesh):
    rows = P("dp", None, "head", None)
    cols = P(None, "head")
    placed = (
        rows, rows, rows, rows, P("dp", None), P(), P(), P(), P(),
        cols, cols, cols, cols, P(None, "head", None), P(None, "head", None), cols, P("head", None),
        P(), P(), cols,
    )
    return jax.shard_map(
        functools.partial(local, mesh.shape["head"], mesh.shape["dp"]),
        mesh=mesh,
        in_specs=placed,
        out_specs=(
            rows, rows, rows, rows, P(), P(), P(),
            cols, cols, cols, cols, P(None, "head", None), P(None, "head", None), cols, P("head", None),
            P(), P(), cols,
        ),
        check_vma=False,
    )
```

```python
import functools
import math

import jax
import jax.numpy as jnp
from jax import lax
from jax.experimental import pallas as pl
from jax.experimental.pallas import tpu as pltpu
from jax.sharding import PartitionSpec as P

HEAD_DIM = 128
WINDOW = 512
BUCKETS = 32
EPSILON = 1e-05
MASKED = -1e30
SCALE = HEAD_DIM ** (-0.5)
F32 = jnp.float32
BF16 = jnp.bfloat16
MIB = 1024 * 1024
COVER = 10**10
LIVE, START, FLIP, PREV = 0, 1, 2, 3
GAIN_TOK, GAIN_STATE, GAIN_MLP, FORGET, ADMIT = 0, 1, 2, 3, 4


def nn(a, b):
    return lax.dot_general(a, b, (((1,), (0,)), ((), ())), preferred_element_type=F32)


def nt(a, b):
    return lax.dot_general(a, b, (((1,), (1,)), ((), ())), preferred_element_type=F32)


def tn(a, b):
    return lax.dot_general(a, b, (((0,), (0,)), ((), ())), preferred_element_type=F32)


def call(body, args, outs, grid=None, in_specs=None, out_specs=None, scratch=(), scalars=0, name=None, vmem=8, cost=COVER):
    smem, whole = pl.BlockSpec(memory_space=pltpu.SMEM), pl.BlockSpec(memory_space=pltpu.VMEM)
    arrays = list(args[scalars:])
    in_specs = list(in_specs or [None] * len(arrays))
    out_specs = list(out_specs or [None] * len(outs))
    outs = list(outs)
    if Order.last is not None:
        arrays[0] = after(arrays[0], Order.last, *Order.arrived)
        Order.arrived = ()
    for k, spec in enumerate(in_specs):
        if spec is not None:
            arrays[k] = pltpu.with_memory_space_constraint(arrays[k], pltpu.HBM)
    for k, spec in enumerate(out_specs):
        if spec is not None:
            outs[k] = pltpu.HBM(outs[k].shape, outs[k].dtype)
    pick = lambda spec: whole if spec is None else pl.BlockSpec(memory_space=pltpu.HBM) if isinstance(spec, str) else spec
    results = pl.pallas_call(
        body,
        out_shape=outs,
        in_specs=[smem] * scalars + [pick(spec) for spec in in_specs],
        out_specs=[pick(spec) for spec in out_specs],
        scratch_shapes=list(scratch),
        compiler_params=pltpu.CompilerParams(vmem_limit_bytes=vmem * MIB),
        cost_estimate=pl.CostEstimate(flops=cost, transcendentals=0, bytes_accessed=0),
        name=name,
        **({"grid": grid} if grid else {}),
    )(*args[:scalars], *arrays)
    Order.last = results[0]
    return results


def after(x, *deps):
    return lax.optimization_barrier((x, *deps))[0]


class Order:
    last = None
    arrived = ()


def arrive(*chunk_lists):
    Order.arrived = (*Order.arrived, *(c[-1] for c in chunk_lists))


def sds(shape, dtype):
    return jax.ShapeDtypeStruct(shape, dtype)


def norm_parts(v):
    mean = jnp.mean(v, axis=-1, keepdims=True)
    cent = v - mean
    var = jnp.mean(cent * cent, axis=-1, keepdims=True)
    inv = lax.rsqrt(var + EPSILON)
    return cent * inv, inv


def norm_back(n, inv, w, g):
    wg = w * g
    return (wg - jnp.mean(wg, -1, keepdims=True) - n * jnp.mean(wg * n, -1, keepdims=True)) * inv


def sum_refs(refs):
    total = refs[0][...].astype(F32)
    for r in refs[1:]:
        total = total + r[...].astype(F32)
    return total


def fetch(pairs, sems):
    copies = [pltpu.make_async_copy(src, dst, sems.at[k]) for k, (src, dst) in enumerate(pairs)]
    for c in copies:
        c.start()
    return copies


def project(chunks, params, gain_at, wq, wk, wv, name):
    count = len(chunks)
    rows, d = chunks[0].shape
    w = wq.shape[1]
    total = rows * count

    def body(*refs):
        xs, p_r, weights, (n_ref, *outs) = refs[:count], refs[count], refs[count + 1 : count + 4], refs[count + 4 : count + 8]
        bufs, sems = refs[count + 8 : count + 11], refs[count + 11]
        copies = fetch(zip(weights, bufs), sems)
        for c in range(count):
            n = xs[c][...]
            if gain_at is not None:
                n = (norm_parts(n.astype(F32))[0] * p_r[gain_at : gain_at + 1, :]).astype(BF16)
            n_ref[c * rows : (c + 1) * rows, :] = n
        for out, buf, copy in zip(outs, bufs, copies):
            copy.wait()
            out[...] = nn(n_ref[...], buf[...]).astype(BF16)

    out = sds((total, w), BF16)
    return call(
        body,
        [*chunks, params, wq, wk, wv],
        [sds((total, d), BF16), out, out, out],
        in_specs=[None] * (count + 1) + ["hbm"] * 3,
        scratch=[pltpu.VMEM((d, w), BF16)] * 3 + [pltpu.SemaphoreType.DMA((3,))],
        name=name,
        vmem=10,
    )


def lanes(h):
    return pl.ds(pl.multiple_of(h * HEAD_DIM, HEAD_DIM), HEAD_DIM)


def softmax_cols(s):
    e = jnp.exp(s - jnp.max(s, axis=0, keepdims=True))
    return (e * (1.0 / jnp.sum(e, axis=0, keepdims=True))).astype(BF16)


def write_parts(value, parts, rows):
    for c, part in enumerate(parts):
        part[...] = value[c * rows : (c + 1) * rows, :].astype(BF16)


def window_masks(flip):
    key_row = lax.broadcasted_iota(jnp.int32, (WINDOW, WINDOW), 0) ^ flip
    query_row = lax.broadcasted_iota(jnp.int32, (WINDOW, WINDOW), 1) ^ flip
    return key_row, query_row


def out_copies(buf, outs, sems, h, slot):
    return [pltpu.make_async_copy(buf.at[slot, k], o.at[h], sems.at[slot, k]) for k, o in enumerate(outs)]


def attend(flags, q, selfs, cross, by_dist, prev, ow, chunks, name):
    t, w = q.shape
    d = ow.shape[2]
    heads = w // HEAD_DIM
    rows = t // chunks
    window = by_dist is not None
    arrays = [q, *selfs, *cross] + ([by_dist] if window else []) + (list(prev) if prev else []) + [ow]

    def body(flags, *refs):
        refs = list(refs)
        q_r, ka_r, va_r, kb_r, vb_r = refs[:5]
        del refs[:5]
        if window:
            f_r = refs.pop(0)
        if prev:
            kp_r, vp_r = refs.pop(0), refs.pop(0)
        ow_r, out_r, pa_o, pb_o = refs[:4]
        parts, (pbuf, sems, obuf, osem) = refs[4:-4], refs[-4:]
        (ow_copy,) = fetch([(ow_r, obuf)], osem)
        flip, prev_ok = flags[FLIP], flags[PREV]

        def step(h, carry):
            slot = h % 2
            at = lanes(h)

            @pl.when(h >= 2)
            def _():
                for c in out_copies(pbuf, (pa_o, pb_o), sems, h - 2, slot):
                    c.wait()

            qv = q_r[:, at]
            s = nt(ka_r[:, at], qv)
            if window:
                key_row, query_row = window_masks(flip)
                tri = allowed = key_row <= query_row
                if prev:
                    s = jnp.where(tri, s, nt(kp_r[:, at], qv))
                    allowed = key_row <= query_row + prev_ok * (2 * WINDOW)
                bias = pltpu.roll(jnp.broadcast_to(f_r[h], (WINDOW, WINDOW)), 0, 1, stride=1, stride_axis=0)
                s = jnp.where(allowed, s * SCALE + bias, MASKED)
            else:
                s = s * SCALE
            p = softmax_cols(s)
            pbuf[slot, 0] = p
            if prev:
                zero = jnp.zeros_like(p)
                o = tn(jnp.where(tri, p, zero), va_r[:, at]) + tn(jnp.where(tri, zero, p), vp_r[:, at])
            else:
                o = tn(p, va_r[:, at])
            out_r[0, :, at] = o.astype(BF16)
            p = softmax_cols(nt(kb_r[:, at], qv) * SCALE)
            pbuf[slot, 1] = p
            out_r[1, :, at] = tn(p, vb_r[:, at]).astype(BF16)
            for c in out_copies(pbuf, (pa_o, pb_o), sems, h, slot):
                c.start()
            return carry

        lax.fori_loop(0, heads, step, 0)
        ow_copy.wait()
        write_parts(nn(out_r[0], obuf[0]) + nn(out_r[1], obuf[1]), parts, rows)
        for h in range(max(0, heads - 2), heads):
            for c in out_copies(pbuf, (pa_o, pb_o), sems, h, h % 2):
                c.wait()

    probs = sds((heads, WINDOW, t), BF16)
    return call(
        body,
        [flags, *arrays],
        [sds((2, t, w), BF16), probs, probs] + [sds((rows, d), BF16)] * chunks,
        in_specs=[None] * (len(arrays) - 1) + ["hbm"],
        out_specs=[None, "hbm", "hbm"] + [None] * chunks,
        scratch=[
            pltpu.VMEM((2, 2, WINDOW, t), BF16),
            pltpu.SemaphoreType.DMA((2, 2)),
            pltpu.VMEM((2, w, d), BF16),
            pltpu.SemaphoreType.DMA((1,)),
        ],
        scalars=1,
        name=name,
        vmem=14,
    )


def score_back(p16, dp):
    p = p16.astype(F32)
    t = p * dp
    return (t - p * jnp.sum(t, axis=0, keepdims=True)).astype(BF16)


def distance_sums(ds):
    x = ds.astype(F32)
    n = WINDOW
    while n > 1:
        n //= 2
        x = x[:n] + pltpu.roll(x[n:], WINDOW - n, 1)
    return x


def attend_back(flags, q, selfs, cross, window, prev, pa, pb, branch, ow, adds, final, name):
    t, w = q.shape
    d = ow.shape[2]
    heads = w // HEAD_DIM
    count = len(branch)
    rows = t // count
    given = [a for a in adds if a is not None]
    arrays = [q, *selfs, *cross] + (list(prev) if prev else []) + [pa, pb, *branch, ow, *given]
    n_first = 7 if prev else 5

    def body(flags, *refs):
        refs = list(refs)
        q_r, ka_r, va_r, kb_r, vb_r = refs[:5]
        del refs[:5]
        if prev:
            kp_r, vp_r = refs.pop(0), refs.pop(0)
        pa_i, pb_i = refs.pop(0), refs.pop(0)
        br = refs[:count]
        ow_r = refs[count]
        del refs[: count + 1]
        add_refs = [None if a is None else refs.pop(0) for a in adds]
        dq_r, dka_r, dva_r, dkb_r, dvb_r = refs[:5]
        del refs[:5]
        if window:
            bd_r = refs.pop(0)
        if prev:
            dkp_r, dvp_r = refs.pop(0), refs.pop(0)
        do_r, pbuf, sems, obuf, osem = refs
        (ow_copy,) = fetch([(ow_r, obuf)], osem)
        flip = flags[FLIP]

        def loads(h, slot):
            return [pltpu.make_async_copy(p.at[h], pbuf.at[slot, k], sems.at[slot, k]) for k, p in enumerate((pa_i, pb_i))]

        for c in loads(0, 0):
            c.start()
        ow_copy.wait()
        for c in range(count):
            for k in range(2):
                do_r[k, c * rows : (c + 1) * rows, :] = nt(br[c][...], obuf[k]).astype(BF16)

        def step(h, carry):
            slot = h % 2
            at = lanes(h)

            @pl.when(h + 1 < heads)
            def _():
                for c in loads(h + 1, 1 - slot):
                    c.start()

            for c in loads(h, slot):
                c.wait()

            def put(ref, value, add):
                if add is not None:
                    value = value + add[:, at].astype(F32)
                ref[:, at] = value.astype(ref.dtype)

            qv, do_a, do_b = q_r[:, at], do_r[0, :, at], do_r[1, :, at]
            p16 = pbuf[slot, 0]
            dp = nt(va_r[:, at], do_a)
            if prev:
                key_row, query_row = window_masks(flip)
                tri = key_row <= query_row
                dp = jnp.where(tri, dp, nt(vp_r[:, at], do_a))
            ds = score_back(p16, dp)
            if window:
                bd_r[h] = distance_sums(ds)
            if prev:
                zero = jnp.zeros_like(ds)
                p_prev, ds_prev = jnp.where(tri, zero, p16), jnp.where(tri, zero, ds)
                p16, ds = jnp.where(tri, p16, zero), jnp.where(tri, ds, zero)
                dvp_r[:, at] = nn(p_prev, do_a)
                dkp_r[:, at] = nn(ds_prev, qv) * SCALE
            put(dva_r, nn(p16, do_a), add_refs[1])
            put(dka_r, nn(ds, qv) * SCALE, add_refs[0])
            dq = tn(ds, ka_r[:, at])
            if prev:
                dq = dq + tn(ds_prev, kp_r[:, at])
            p16 = pbuf[slot, 1]
            ds = score_back(p16, nt(vb_r[:, at], do_b))
            put(dvb_r, nn(p16, do_b), add_refs[3])
            put(dkb_r, nn(ds, qv) * SCALE, add_refs[2])
            dq = dq + tn(ds, kb_r[:, at])
            dq_r[:, at] = (dq * SCALE).astype(BF16)
            return carry

        lax.fori_loop(0, heads, step, 0)

    full = lambda dt: sds((t, w), dt)
    outs = [full(BF16), full(final[0]), full(final[0]), full(final[1]), full(final[1])]
    if window:
        outs.append(sds((heads, 1, WINDOW), F32))
    if prev:
        outs += [full(F32)] * 2
    return call(
        body,
        [flags, *arrays],
        outs,
        in_specs=[None] * n_first + ["hbm"] * 2 + [None] * count + ["hbm"] + [None] * len(given),
        scratch=[
            pltpu.VMEM((2, t, w), BF16),
            pltpu.VMEM((2, 2, WINDOW, t), BF16),
            pltpu.SemaphoreType.DMA((2, 2)),
            pltpu.VMEM((2, w, d), BF16),
            pltpu.SemaphoreType.DMA((1,)),
        ],
        scalars=1,
        name=name,
        vmem=14,
    )


def project_back(dq, dk, dv, wq, wk, wv, chunks, name):
    t, w = dq.shape
    d = wq.shape[0]
    rows = t // chunks

    def body(*refs):
        grads, weights, parts, bufs, sems = refs[:3], refs[3:6], refs[6:-4], refs[-4:-1], refs[-1]
        copies = fetch(zip(weights, bufs), sems)
        for c in copies:
            c.wait()
        for c, part in enumerate(parts):
            at = slice(c * rows, (c + 1) * rows)
            total = nt(grads[0][at, :], bufs[0][...])
            for g, buf in zip(grads[1:], bufs[1:]):
                total = total + nt(g[at, :], buf[...])
            part[...] = total.astype(BF16)

    return call(
        body,
        [dq, dk, dv, wq, wk, wv],
        [sds((rows, d), BF16)] * chunks,
        in_specs=[None] * 3 + ["hbm"] * 3,
        scratch=[pltpu.VMEM((d, w), BF16)] * 3 + [pltpu.SemaphoreType.DMA((3,))],
        name=name,
        vmem=10,
    )


def feed_forward(normed, cots, w_in, w_out, name):
    count = len(normed)
    rows, d = normed[0].shape
    f = w_in.shape[1]
    tile = min(f, 512)
    t = rows * count
    c0 = math.sqrt(2.0 / math.pi)

    def body(*refs):
        nm, og = refs[:count], refs[count : 2 * count]
        wi_r, wo_r, hid_r, pre_r = refs[2 * count : 2 * count + 4]
        rest = refs[2 * count + 4 :]
        parts_y, parts_g, (acc_y, acc_g, ibuf, obuf, sems) = rest[:count], rest[count : 2 * count], rest[-5:]

        def loads(i, slot):
            cols = pl.ds(pl.multiple_of(i * tile, tile), tile)
            return [
                pltpu.make_async_copy(wi_r.at[:, cols], ibuf.at[slot], sems.at[slot, 0]),
                pltpu.make_async_copy(wo_r.at[cols, :], obuf.at[slot], sems.at[slot, 1]),
            ]

        for c in loads(0, 0):
            c.start()
        acc_y[...] = jnp.zeros_like(acc_y)
        acc_g[...] = jnp.zeros_like(acc_g)

        def step(i, carry):
            cols = pl.ds(pl.multiple_of(i * tile, tile), tile)
            slot = i % 2

            @pl.when(i + 1 < f // tile)
            def _():
                for c in loads(i + 1, 1 - slot):
                    c.start()

            for c in loads(i, slot):
                c.wait()
            wi, wo = ibuf[slot], obuf[slot]
            for c in range(count):
                at = slice(c * rows, (c + 1) * rows)
                v = nn(nm[c][...], wi)
                sq = v * v
                th = jnp.tanh(v * (c0 + c0 * 0.044715 * sq))
                half = 0.5 + 0.5 * th
                hidden = (v * half).astype(BF16)
                slope = half + (0.5 * v) * (1.0 - th * th) * (c0 + 3.0 * c0 * 0.044715 * sq)
                hid_r[at, cols] = hidden
                pre = (nt(og[c][...], wo) * slope).astype(BF16)
                pre_r[at, cols] = pre
                acc_y[at, :] += nn(hidden, wo)
                acc_g[at, :] += nt(pre, wi)
            return carry

        lax.fori_loop(0, f // tile, step, 0)
        write_parts(acc_y, parts_y, rows)
        write_parts(acc_g, parts_g, rows)

    return call(
        body,
        [*normed, *cots, w_in, w_out],
        [sds((t, f), BF16)] * 2 + [sds((rows, d), BF16)] * (2 * count),
        in_specs=[None] * (2 * count) + ["hbm"] * 2,
        scratch=[pltpu.VMEM((t, d), F32)] * 2
        + [pltpu.VMEM((2, d, tile), BF16), pltpu.VMEM((2, tile, d), BF16), pltpu.SemaphoreType.DMA((2, 2))],
        name=name,
        vmem=18,
    )


def row_call(body, flags, arrays, outs, name, cost=0):
    n_in = len(arrays)

    def wrapped(flags, *refs):
        values = body(flags, *refs[:n_in])
        for o, v in zip(refs[n_in:], values):
            o[...] = jnp.sum(v, 0, keepdims=True) if o.shape[0] == 1 else v.astype(o.dtype)

    return call(wrapped, [flags, *arrays], outs, scalars=1, name=name, cost=cost)


def f32(ref):
    return ref[...].astype(F32)


def param(p_r, at):
    return p_r[at : at + 1, :]


def mid_norm(flags, tok, adds, params, name):
    def body(flags, tok_r, p_r, *adds_r):
        mid = f32(tok_r) + sum_refs(adds_r)
        return mid, norm_parts(mid)[0] * param(p_r, GAIN_MLP)

    return row_call(body, flags, [tok, params, *adds], [sds(tok.shape, F32), sds(tok.shape, BF16)], name)


def state_step(flags, first, second, adds, params, name):
    def body(flags, a_r, b_r, p_r, *adds_r):
        upd = sum_refs(adds_r)
        car = param(p_r, FORGET) * f32(a_r) + param(p_r, ADMIT) * upd
        st = jnp.where(flags[START].astype(F32) > 0.5, f32(b_r), car)
        return upd, car, st, norm_parts(st)[0] * param(p_r, GAIN_STATE)

    full = sds(first.shape, F32)
    arrays = [first, second, params, *adds]
    return row_call(body, flags, arrays, [full, full, full, sds(first.shape, BF16)], name)


def mid_back(flags, mid, params, cot, adds, name, cost=0):
    def body(flags, mid_r, p_r, cot_r, *adds_r):
        n, inv = norm_parts(mid_r[...])
        g = sum_refs(adds_r)
        mg = f32(cot_r) + norm_back(n, inv, param(p_r, GAIN_MLP), g)
        return mg, mg, g * n

    outs = [sds(mid.shape, F32), sds(mid.shape, BF16), sds((1, mid.shape[1]), F32)]
    return row_call(body, flags, [mid, params, cot, *adds], outs, name, cost)


def token_back(flags, live_at, tok, params, mg, cot, adds, name):
    def body(flags, tok_r, p_r, mg_r, cot_r, *adds_r):
        n, inv = norm_parts(f32(tok_r))
        g = sum_refs(adds_r)
        row = mg_r[...] + norm_back(n, inv, param(p_r, GAIN_TOK), g)
        if live_at is not None:
            row = jnp.where(flags[live_at].astype(F32) > 0.5, row, f32(cot_r))
        return row, g * n

    outs = [sds(tok.shape, F32), sds((1, tok.shape[1]), F32)]
    return row_call(body, flags, [tok, params, mg, cot, *adds], outs, name)


def gate_terms(snc, upd, state, p_r):
    sf, si = param(p_r, FORGET), param(p_r, ADMIT)
    return sf, si, snc * state * (sf * (1.0 - sf)), snc * upd * (si * (1.0 - si))


def state_back_second(flags, state, params, cot0, cot1, upd, adds, name):
    n_upd = len(upd)

    def body(flags, st_r, p_r, c0_r, c1_r, *rest):
        upd_v, adds_r = sum_refs(rest[:n_upd]), rest[n_upd:]
        live = flags[LIVE].astype(F32)
        start = flags[START].astype(F32)
        c0, c1 = f32(c0_r), f32(c1_r)
        snc = jnp.where(start > 0.5, c1, c0) * live
        st = st_r[...]
        n, inv = norm_parts(st)
        g = sum_refs(adds_r)
        sf, si, gf, gi = gate_terms(snc, upd_v, st, p_r)
        back = jnp.where(live > 0.5, sf * snc + norm_back(n, inv, param(p_r, GAIN_STATE), g), snc)
        snc0 = jnp.where(start > 0.5, c0, back)
        return jnp.where(start * live > 0.5, back, c1), snc0, si * snc0, g * n, gf, gi

    full, row = sds(state.shape, F32), sds((1, state.shape[1]), F32)
    arrays = [state, params, cot0, cot1, *upd, *adds]
    return row_call(body, flags, arrays, [full, full, sds(state.shape, BF16), row, row, row], name)


def state_back_first(flags, state, params, snc, upd, adds, name):
    def body(flags, st_r, p_r, snc_r, upd_r, *adds_r):
        st = f32(st_r)
        n, inv = norm_parts(st)
        g = sum_refs(adds_r)
        snc = snc_r[...]
        sf, _, gf, gi = gate_terms(snc, upd_r[...], st, p_r)
        return sf * snc + norm_back(n, inv, param(p_r, GAIN_STATE), g), g * n, gf, gi

    full, row = sds(state.shape, F32), sds((1, state.shape[1]), F32)
    arrays = [state, params, snc, upd, *adds]
    return row_call(body, flags, arrays, [full, row, row, row], name)


def piece_positions(index, size, order):
    rel = jnp.arange(size, dtype=jnp.int32) ^ index
    pos = jnp.zeros((size,), jnp.int32)
    for bit in order:
        pos = pos * 2 + ((rel >> bit) & 1)
    return pos


def weight_grads(table, jobs, size, name, cost=COVER):
    width = lambda a: a.shape[-1] * (2 if a.ndim == 3 else 1)
    first = lambda b: b[0] if isinstance(b, tuple) else b
    m = width(jobs[0][0][0])
    assert all(width(a) == m for lhs, _ in jobs for a in lhs)
    cols = [first(rhs[0][0]).shape[1] for _, rhs in jobs]
    n = sum(cols)
    tile = min([256] + [a.shape[-1] for lhs, _ in jobs for a in lhs])
    flat, plan = [], []

    def add(a):
        for k, b in enumerate(flat):
            if b is a:
                return k
        flat.append(a)
        return len(flat) - 1

    for lhs, rhs in jobs:
        parts = []
        for a, group in zip(lhs, rhs):
            at, row = add(a), 0
            for b in group:
                b, start, count = b if isinstance(b, tuple) else (b, 0, b.shape[0])
                parts.append((at, row, count, add(b), start))
                row += count
            assert row == a.shape[-2]
        plan.append(parts)
    shapes = [a.shape for a in flat]
    piece = m // size
    half = size // 2

    def body(*refs):
        table, refs = (None, refs) if len(refs) == len(flat) + 1 else (refs[0], refs[1:])

        def step(i, carry):
            col = 0
            for parts, width in zip(plan, cols):
                total = None
                for at, row, count, other, start in parts:
                    if len(shapes[at]) == 3:
                        blocks = shapes[at][2] // tile
                        here = pl.ds(pl.multiple_of((i % blocks) * tile, tile), tile)
                        a = refs[at][i // blocks, row : row + count, here]
                    else:
                        a = refs[at][row : row + count, pl.ds(pl.multiple_of(i * tile, tile), tile)]
                    term = tn(a, refs[other][start : start + count, :])
                    total = term if total is None else total + term
                out = total.astype(BF16)
                if table is None:
                    refs[-1][pl.ds(pl.multiple_of(i * tile, tile), tile), col : col + width] = out
                else:
                    keep, send = refs[-2:]
                    for j in range(tile // piece):
                        pos = table[i * (tile // piece) + j]
                        part = out[j * piece : (j + 1) * piece, :]

                        @pl.when(pos < half)
                        def _():
                            keep[pos, :, col : col + width] = part

                        @pl.when(pos >= half)
                        def _():
                            send[pos - half, :, col : col + width] = part

                col += width
            return carry

        lax.fori_loop(0, m // tile, step, 0)

    if table is None:
        outs = [sds((m, n), BF16)]
    else:
        outs = [sds((half, piece, n), BF16)] * 2
    args = flat if table is None else [table, *flat]
    return call(body, args, outs, scalars=len(args) - len(flat), name=name, vmem=12, cost=cost), cols


def split_rows(a, count):
    rows = a.shape[0] // count
    return [(a, k * rows, rows) for k in range(count)]


def widen(a, name):
    rows, n = a.shape
    tile = min(rows, 256)
    spec = pl.BlockSpec((tile, n), lambda i: (i, 0))

    def body(a_r, o_r):
        o_r[...] = a_r[...].astype(F32)

    return call(body, [a], [sds(a.shape, F32)], grid=(rows // tile,), in_specs=[spec], out_specs=[spec], name=name)[0]


def flip_dp(x, bit, size):
    return lax.ppermute(x, "dp", [(i, i ^ (1 << bit)) for i in range(size)])


def add_pair(a, b):
    return (a.astype(F32) + b.astype(F32)).astype(BF16)


def in_turn(x):
    return x if Order.last is None else after(x, Order.last)


def sum_pieces(pair, size, order):
    keep, send = pair
    got = flip_dp(send, order[0], size)
    yield
    for bit in order[1:]:
        half = keep.shape[0] // 2
        got = in_turn(got)
        keep, send = add_pair(keep[:half], got[:half]), add_pair(keep[half:], got[half:])
        Order.last = send
        got = flip_dp(send, bit, size)
        yield
    whole = add_pair(keep, in_turn(got))
    for bit in reversed(order[1:]):
        Order.last = whole
        got = flip_dp(whole, bit, size)
        yield
        whole = jnp.concatenate([whole, in_turn(got)], 0)
    Order.last = whole
    got = flip_dp(whole, order[0], size)
    yield
    yield whole, got


def sum_small(x, size, order):
    for bit in order:
        got = flip_dp(x, bit, size)
        yield
        x = x + in_turn(got)
        Order.last = x
    yield x


def place_pieces(table, own, other, widths, name):
    half, piece, n = own.shape
    size = 2 * half
    per = max(1, 256 // piece)

    def body(table, own_r, other_r, *outs):
        for j in range(per):
            pos = table[pl.program_id(0) * per + j]
            rows = slice(j * piece, (j + 1) * piece)

            def put(src, at):
                start = 0
                for o, width in zip(outs, widths):
                    o[rows, :] = src[at, :, start : start + width].astype(F32)
                    start += width

            @pl.when(pos < half)
            def _():
                put(own_r, pos)

            @pl.when(pos >= half)
            def _():
                put(other_r, pos - half)

    return call(
        body,
        [table, own, other],
        [sds((size * piece, width), F32) for width in widths],
        grid=(size // per,),
        in_specs=[pl.BlockSpec(own.shape, lambda i: (0, 0, 0), pipeline_mode=pl.Buffered(1))] * 2,
        out_specs=[pl.BlockSpec((per * piece, width), lambda i: (i, 0)) for width in widths],
        scalars=1,
        name=name,
        vmem=24,
    )


def local(
    head_size,
    dp_size,
    tokens,
    out_grad,
    init_state,
    state_grad,
    seq_blocks,
    bucket_table,
    gain_tok,
    gain_state,
    gain_mlp,
    query_tok,
    query_state,
    key_weight,
    value_weight,
    out_tok,
    out_state,
    mlp_in,
    mlp_out,
    gate_forget,
    gate_input,
    rel_bias,
):
    paired = head_size == 2
    chunks = 2 if paired else 1
    rows = tokens.shape[2]
    width = query_tok.shape[1]
    heads = width // HEAD_DIM

    def exchange(x):
        return lax.ppermute(x, "head", [(0, 1), (1, 0)])

    def gather(x):
        return (x, exchange(x)) if paired else (lax.all_gather(x, "head", axis=0, tiled=True),)

    def scatter(parts):
        if paired:
            return (parts[0], exchange(parts[1]))
        return (lax.psum_scatter(parts[0], "head", scatter_dimension=0, tiled=True),)

    first_len = seq_blocks[0, 0]
    live1 = (seq_blocks[0, 0] + seq_blocks[0, 1] > 1).astype(jnp.int32)
    start1 = (first_len == 1).astype(jnp.int32)
    flip = lax.axis_index("head") * rows if paired else jnp.int32(0)
    flags = jnp.stack([live1, start1, flip.astype(jnp.int32), 1 - start1])
    is_live, is_start = live1 > 0, start1 > 0

    onehot = (bucket_table[:, None] == jnp.arange(BUCKETS, dtype=jnp.int32)[None, :]).astype(F32)
    by_dist = jnp.dot(rel_bias.T, onehot.T, precision=lax.Precision.HIGHEST)[:, None, :]

    tok = [tokens[0, 0], tokens[0, 1]]
    init = [init_state[0, 0], init_state[0, 1]]
    cot = [out_grad[0, 0], out_grad[0, 1]]
    scot = [state_grad[0, 0], state_grad[0, 1]]
    live_cot = [cot[0], jnp.where(is_live, cot[1], jnp.zeros_like(cot[1]))]

    admit, forget = jax.nn.sigmoid(gate_input), jax.nn.sigmoid(gate_forget)
    bits = tuple(range(dp_size.bit_length() - 1))
    orders = (bits, bits[:1] + bits[2:] + bits[1:2])
    tables = [piece_positions(lax.axis_index("dp"), dp_size, order) for order in orders]
    add_all = lambda adds: functools.reduce(jnp.add, [a.astype(F32) for a in adds])
    hold = lambda parts, dep: [*parts[:-1], after(parts[-1], dep)]
    Order.last, Order.arrived = None, ()
    params = jnp.stack([gain_tok, gain_state, gain_mlp, forget, admit])
    params = jnp.concatenate([params, jnp.zeros((3, params.shape[1]), F32)], 0)

    def weight_sum(which, jobs, name):
        rows_of = lambda job: job[0][0].shape[-1] * (2 if job[0][0].ndim == 3 else 1)
        groups = {}
        for k, job in enumerate(jobs):
            groups.setdefault(rows_of(job), []).append(k)
        steps, cols = [], []
        for m, members in groups.items():
            pair, width = weight_grads(tables[which], [jobs[k] for k in members], dp_size, name)
            steps.append(sum_pieces(pair, dp_size, orders[which]))
            next(steps[-1])
            cols.append(width)
        return dict(steps=steps, which=which, cols=cols, members=list(groups.values()), name=name, pieces=None, grads=None)

    def advance(*sums):
        for w in sums:
            brought = [next(steps) for steps in w["steps"]]
            if brought[0] is not None:
                w["pieces"] = brought

    def place(w):
        grads = {}
        for members, pieces, cols in zip(w["members"], w["pieces"], w["cols"]):
            for k, grad in zip(members, place_pieces(tables[w["which"]], *pieces, cols, "pl_" + w["name"])):
                grads[k] = grad
        w["grads"] = [grads[k] for k in sorted(grads)]

    tok0_all, st0_all, tok1_all, cot1_all = gather(tok[0]), gather(init[0]), gather(tok[1]), gather(live_cot[1])
    nt0, qt0, kt0, vt0 = project(tok0_all, params, GAIN_TOK, query_tok, key_weight, value_weight, "proj_tok0")
    ns0, qs0, ks0, vs0 = project(st0_all, params, GAIN_STATE, query_state, key_weight, value_weight, "proj_state0")
    os0, pss0, psc0, *sparts = attend(
        flags, qs0, (ks0, vs0), (kt0, vt0), None, None, out_state, chunks, "att_state0"
    )
    sadds0 = scatter(sparts)
    nt1, qt1, kt1, vt1 = project(tok1_all, params, GAIN_TOK, query_tok, key_weight, value_weight, "proj_tok1")
    upd0, carried0, state1, sn1 = state_step(
        flags, init[0], init[1], sadds0, params, "state_step0"
    )
    sn1_all = gather(sn1)
    cot0_all = gather(after(live_cot[0], sn1))
    ot0, pts0, ptc0, *tparts = attend(
        flags, qt0, (kt0, vt0), (ks0, vs0), by_dist, None, out_tok, chunks, "att_tok0"
    )
    tadds0 = scatter(tparts)
    arrive(cot1_all)
    ns1, qs1, ks1, vs1 = project(sn1_all, params, None, query_state, key_weight, value_weight, "proj_state1")
    ot1, pts1, ptc1, *tparts = attend(
        flags, qt1, (kt1, vt1), (ks1, vs1), by_dist, (kt0, vt0), out_tok, chunks, "att_tok1"
    )
    tadds1 = scatter(tparts)
    mid0, nm0 = mid_norm(flags, tok[0], tadds0, params, "mid0")
    nm0_all = gather(nm0)
    arrive(cot0_all)
    os1, pss1, psc1, *sparts1 = attend(
        flags, qs1, (ks1, vs1), (kt1, vt1), None, None, out_state, chunks, "att_state1"
    )
    mid1, nm1 = mid_norm(flags, tok[1], tadds1, params, "mid1")
    nm1_all = gather(nm1)
    snc1 = jnp.where(is_start, scot[1], scot[0]).astype(F32) * live1.astype(F32)
    hid0, pre0, *mparts0 = feed_forward(nm0_all, cot0_all, mlp_in, mlp_out, "ff0")
    gadds0 = scatter(mparts0[chunks:])
    ug1_all = gather(after((admit * snc1).astype(BF16), hid0))
    hid1, pre1, *mparts1 = feed_forward(nm1_all, cot1_all, mlp_in, mlp_out, "ff1")
    gadds1 = scatter(mparts1[chunks:])

    (g_in,), _ = weight_grads(
        None, [([*nm0_all, *nm1_all], [[p] for p in split_rows(pre0, chunks) + split_rows(pre1, chunks)])], dp_size, "wg_in"
    )
    arrive(ug1_all)
    (g_out,), _ = weight_grads(None, [([hid0, hid1], [cot0_all, cot1_all])], dp_size, "wg_out", 0)
    d_in, d_out = lax.psum((g_in, g_out), "dp")
    mg1, mg16b, gm1 = mid_back(flags, mid1, params, live_cot[1], gadds1, "mid_back1")
    mg1_all = gather(mg16b)
    mg0, mg16, gm0 = mid_back(flags, mid0, params, live_cot[0], gadds0, "mid_back0")
    mg0_all = gather(mg16)
    dqs1, dks1, dvs1, dkt1, dvt1 = attend_back(
        flags, qs1, (ks1, vs1), (kt1, vt1), False, None, pss1, psc1, ug1_all, out_state, [None] * 4, (F32, F32), "att_state_back1"
    )
    sadds1 = scatter(hold(sparts1, dqs1))
    dqt1, dkt1, dvt1, dks1, dvs1, bd1, dkp, dvp = attend_back(
        flags, qt1, (kt1, vt1), (ks1, vs1), True, (kt0, vt0), pts1, ptc1, mg1_all, out_tok,
        [dkt1, dvt1, dks1, dvs1], (BF16, BF16), "att_tok_back1",
    )
    sback1 = project_back(dqs1, dks1, dvs1, query_state, key_weight, value_weight, chunks, "pb_state1")
    sback1 = scatter(sback1)
    dqt0, dkt0, dvt0, dks0, dvs0, bd0 = attend_back(
        flags, qt0, (kt0, vt0), (ks0, vs0), True, None, pts0, ptc0, mg0_all, out_tok,
        [dkp, dvp, None, None], (F32, F32), "att_tok_back0",
    )
    ig1, snc0, ug0, gs1, gf1, gi1 = state_back_second(
        flags, state1, params, scot[0], scot[1], sadds1, sback1, "state_back1"
    )
    ug0_all = gather(ug0)
    w_early = weight_sum(0, [([ot0, ot1], [mg0_all, mg1_all]), ([nt0, nt1], [[dqt0], [dqt1]])], "wg_early")
    madds0 = scatter(hold(mparts0[:chunks], ug0_all[-1]))
    madds1 = scatter(hold(mparts1[:chunks], ug0_all[-1]))
    dqs0, dks0, dvs0, dkt0, dvt0 = attend_back(
        flags, qs0, (ks0, vs0), (kt0, vt0), False, None, pss0, psc0, ug0_all, out_state,
        [dks0, dvs0, dkt0, dvt0], (BF16, BF16), "att_state_back0",
    )
    advance(w_early)
    sback0 = project_back(dqs0, dks0, dvs0, query_state, key_weight, value_weight, chunks, "pb_state0")
    sback0 = scatter(sback0)
    normed_all = [nt0, nt1, ns0, ns1]
    w_kv = weight_sum(
        0, [(normed_all, [[dkt0], [dkt1], [dks0], [dks1]]), (normed_all, [[dvt0], [dvt1], [dvs0], [dvs1]])], "wg_kv"
    )
    w_late = weight_sum(0, [([os0, os1], [ug0_all, ug1_all]), ([ns0, ns1], [[dqs0], [dqs1]])], "wg_late")
    advance(w_early, w_kv)
    arrive(madds0, madds1)
    tback0 = project_back(dqt0, dkt0, dvt0, query_tok, key_weight, value_weight, chunks, "pb_tok0")
    tback0 = scatter(tback0)
    tback1 = project_back(dqt1, dkt1, dvt1, query_tok, key_weight, value_weight, chunks, "pb_tok1")
    tback1 = scatter(tback1)
    advance(w_late)
    ig0, gs0, gf0, gi0 = state_back_first(
        flags, init[0], params, snc0, upd0, sback0, "state_back0"
    )
    row0, gt0 = token_back(flags, None, tok[0], params, mg0, cot[0], tback0, "tok_back0")
    row1, gt1 = token_back(flags, LIVE, tok[1], params, mg1, cot[1], tback1, "tok_back1")

    rel = jnp.dot((bd0 + bd1)[:, 0, :], onehot, precision=lax.Precision.HIGHEST)
    small = jnp.concatenate([gt0 + gt1, gs0 + gs1, gm0 + gm1, gf0 + gf1, gi0 + gi1], 0)
    small = small + exchange(small) if paired else lax.psum(small, "head")
    d = small.shape[1]
    rel_row = jnp.pad(rel.reshape(1, -1), ((0, 0), (0, d - heads * BUCKETS)))
    small = jnp.concatenate([small, rel_row, jnp.zeros((2, d), F32)], 0)
    w_small = dict(steps=[sum_small(small, dp_size, bits)], pieces=None)

    running = [w_early, w_kv, w_late, w_small]
    while running:
        advance(*running)
        for w in list(running):
            if w["pieces"] is not None:
                running.remove(w)
                if w is not w_small:
                    place(w)
    (d_ot, d_qt), (d_k, d_v), (d_os, d_qs) = w_early["grads"], w_kv["grads"], w_late["grads"]
    (small,) = w_small["pieces"]
    d_in, d_out = widen(d_in, "widen_in"), widen(d_out, "widen_out")
    d_rel = small[5, : heads * BUCKETS].reshape(heads, BUCKETS).T

    new0 = (mid0 + add_all(madds0)).astype(BF16)
    new1 = jnp.where(is_live, (mid1 + add_all(madds1)).astype(BF16), tok[1])
    carried1 = jnp.where(is_live, forget * state1 + admit * add_all(sadds1), state1)
    next0 = jnp.where(is_start, carried0, carried1)
    next1 = jnp.where(is_start & is_live, carried1, init[1].astype(F32))

    return (
        jnp.stack([new0, new1])[None],
        jnp.stack([next0, next1])[None],
        jnp.stack([row0, row1])[None],
        jnp.stack([ig0, ig1])[None],
        small[0],
        small[1],
        small[2],
        d_qt,
        d_qs,
        d_k,
        d_v,
        d_ot.reshape(out_tok.shape),
        d_os.reshape(out_state.shape),
        d_in,
        d_out,
        small[3],
        small[4],
        d_rel,
    )


def solution(mesh):
    rows = P("dp", None, "head", None)
    cols = P(None, "head")
    placed = (
        rows, rows, rows, rows, P("dp", None), P(), P(), P(), P(),
        cols, cols, cols, cols, P(None, "head", None), P(None, "head", None), cols, P("head", None),
        P(), P(), cols,
    )
    return jax.shard_map(
        functools.partial(local, mesh.shape["head"], mesh.shape["dp"]),
        mesh=mesh,
        in_specs=placed,
        out_specs=(
            rows, rows, rows, rows, P(), P(), P(),
            cols, cols, cols, cols, P(None, "head", None), P(None, "head", None), cols, P("head", None),
            P(), P(), cols,
        ),
        check_vma=False,
    )
```

```python
import functools
import math

import jax
import jax.numpy as jnp
from jax import lax
from jax.experimental import pallas as pl
from jax.experimental.pallas import tpu as pltpu
from jax.sharding import PartitionSpec as P

HEAD_DIM = 128
WINDOW = 512
BUCKETS = 32
EPSILON = 1e-05
MASKED = -1e30
SCALE = HEAD_DIM ** (-0.5)
F32 = jnp.float32
BF16 = jnp.bfloat16
MIB = 1024 * 1024
COVER = 10**10
LIVE, START, FLIP, PREV = 0, 1, 2, 3
GAIN_TOK, GAIN_STATE, GAIN_MLP, FORGET, ADMIT = 0, 1, 2, 3, 4


def nn(a, b):
    return lax.dot_general(a, b, (((1,), (0,)), ((), ())), preferred_element_type=F32)


def nt(a, b):
    return lax.dot_general(a, b, (((1,), (1,)), ((), ())), preferred_element_type=F32)


def tn(a, b):
    return lax.dot_general(a, b, (((0,), (0,)), ((), ())), preferred_element_type=F32)


def call(body, args, outs, grid=None, in_specs=None, out_specs=None, scratch=(), scalars=0, name=None, vmem=8, cost=COVER):
    smem, whole = pl.BlockSpec(memory_space=pltpu.SMEM), pl.BlockSpec(memory_space=pltpu.VMEM)
    arrays = list(args[scalars:])
    in_specs = list(in_specs or [None] * len(arrays))
    out_specs = list(out_specs or [None] * len(outs))
    outs = list(outs)
    if Order.last is not None:
        arrays[0] = after(arrays[0], Order.last, *Order.arrived)
        Order.arrived = ()
    for k, spec in enumerate(in_specs):
        if spec is not None:
            arrays[k] = pltpu.with_memory_space_constraint(arrays[k], pltpu.HBM)
    for k, spec in enumerate(out_specs):
        if spec is not None:
            outs[k] = pltpu.HBM(outs[k].shape, outs[k].dtype)
    pick = lambda spec: whole if spec is None else pl.BlockSpec(memory_space=pltpu.HBM) if isinstance(spec, str) else spec
    results = pl.pallas_call(
        body,
        out_shape=outs,
        in_specs=[smem] * scalars + [pick(spec) for spec in in_specs],
        out_specs=[pick(spec) for spec in out_specs],
        scratch_shapes=list(scratch),
        compiler_params=pltpu.CompilerParams(vmem_limit_bytes=vmem * MIB),
        cost_estimate=pl.CostEstimate(flops=cost, transcendentals=0, bytes_accessed=0),
        name=name,
        **({"grid": grid} if grid else {}),
    )(*args[:scalars], *arrays)
    Order.last = results[0]
    return results


def after(x, *deps):
    return lax.optimization_barrier((x, *deps))[0]


class Order:
    last = None
    arrived = ()


def arrive(*chunk_lists):
    Order.arrived = (*Order.arrived, *(c[-1] for c in chunk_lists))


def sds(shape, dtype):
    return jax.ShapeDtypeStruct(shape, dtype)


def norm_parts(v):
    mean = jnp.mean(v, axis=-1, keepdims=True)
    cent = v - mean
    var = jnp.mean(cent * cent, axis=-1, keepdims=True)
    inv = lax.rsqrt(var + EPSILON)
    return cent * inv, inv


def norm_back(n, inv, w, g):
    wg = w * g
    return (wg - jnp.mean(wg, -1, keepdims=True) - n * jnp.mean(wg * n, -1, keepdims=True)) * inv


def sum_refs(refs):
    total = refs[0][...].astype(F32)
    for r in refs[1:]:
        total = total + r[...].astype(F32)
    return total


def fetch(pairs, sems):
    copies = [pltpu.make_async_copy(src, dst, sems.at[k]) for k, (src, dst) in enumerate(pairs)]
    for c in copies:
        c.start()
    return copies


def project(chunks, params, gain_at, wq, wk, wv, name):
    count = len(chunks)
    rows, d = chunks[0].shape
    w = wq.shape[1]
    total = rows * count

    def body(*refs):
        xs, p_r, weights, (n_ref, *outs) = refs[:count], refs[count], refs[count + 1 : count + 4], refs[count + 4 : count + 8]
        bufs, sems = refs[count + 8 : count + 11], refs[count + 11]
        copies = fetch(zip(weights, bufs), sems)
        for c in range(count):
            n = xs[c][...]
            if gain_at is not None:
                n = (norm_parts(n.astype(F32))[0] * p_r[gain_at : gain_at + 1, :]).astype(BF16)
            n_ref[c * rows : (c + 1) * rows, :] = n
        for out, buf, copy in zip(outs, bufs, copies):
            copy.wait()
            out[...] = nn(n_ref[...], buf[...]).astype(BF16)

    out = sds((total, w), BF16)
    return call(
        body,
        [*chunks, params, wq, wk, wv],
        [sds((total, d), BF16), out, out, out],
        in_specs=[None] * (count + 1) + ["hbm"] * 3,
        scratch=[pltpu.VMEM((d, w), BF16)] * 3 + [pltpu.SemaphoreType.DMA((3,))],
        name=name,
        vmem=10,
    )


def lanes(h):
    return pl.ds(pl.multiple_of(h * HEAD_DIM, HEAD_DIM), HEAD_DIM)


def softmax_cols(s):
    e = jnp.exp(s - jnp.max(s, axis=0, keepdims=True))
    return (e * (1.0 / jnp.sum(e, axis=0, keepdims=True))).astype(BF16)


def write_parts(value, parts, rows):
    for c, part in enumerate(parts):
        part[...] = value[c * rows : (c + 1) * rows, :].astype(BF16)


def window_masks(flip):
    key_row = lax.broadcasted_iota(jnp.int32, (WINDOW, WINDOW), 0) ^ flip
    query_row = lax.broadcasted_iota(jnp.int32, (WINDOW, WINDOW), 1) ^ flip
    return key_row, query_row


def out_copies(buf, outs, sems, h, slot):
    return [pltpu.make_async_copy(buf.at[slot, k], o.at[h], sems.at[slot, k]) for k, o in enumerate(outs)]


def attend(flags, q, selfs, cross, by_dist, prev, ow, chunks, name):
    t, w = q.shape
    d = ow.shape[2]
    heads = w // HEAD_DIM
    rows = t // chunks
    window = by_dist is not None
    arrays = [q, *selfs, *cross] + ([by_dist] if window else []) + (list(prev) if prev else []) + [ow]

    def body(flags, *refs):
        refs = list(refs)
        q_r, ka_r, va_r, kb_r, vb_r = refs[:5]
        del refs[:5]
        if window:
            f_r = refs.pop(0)
        if prev:
            kp_r, vp_r = refs.pop(0), refs.pop(0)
        ow_r, out_r, pa_o, pb_o = refs[:4]
        parts, (pbuf, sems, obuf, osem) = refs[4:-4], refs[-4:]
        (ow_copy,) = fetch([(ow_r, obuf)], osem)
        flip, prev_ok = flags[FLIP], flags[PREV]

        def step(h, carry):
            slot = h % 2
            at = lanes(h)

            @pl.when(h >= 2)
            def _():
                for c in out_copies(pbuf, (pa_o, pb_o), sems, h - 2, slot):
                    c.wait()

            qv = q_r[:, at]
            s = nt(ka_r[:, at], qv)
            if window:
                key_row, query_row = window_masks(flip)
                tri = allowed = key_row <= query_row
                if prev:
                    s = jnp.where(tri, s, nt(kp_r[:, at], qv))
                    allowed = key_row <= query_row + prev_ok * (2 * WINDOW)
                bias = pltpu.roll(jnp.broadcast_to(f_r[h], (WINDOW, WINDOW)), 0, 1, stride=1, stride_axis=0)
                s = jnp.where(allowed, s * SCALE + bias, MASKED)
            else:
                s = s * SCALE
            p = softmax_cols(s)
            pbuf[slot, 0] = p
            if prev:
                zero = jnp.zeros_like(p)
                o = tn(jnp.where(tri, p, zero), va_r[:, at]) + tn(jnp.where(tri, zero, p), vp_r[:, at])
            else:
                o = tn(p, va_r[:, at])
            out_r[0, :, at] = o.astype(BF16)
            p = softmax_cols(nt(kb_r[:, at], qv) * SCALE)
            pbuf[slot, 1] = p
            out_r[1, :, at] = tn(p, vb_r[:, at]).astype(BF16)
            for c in out_copies(pbuf, (pa_o, pb_o), sems, h, slot):
                c.start()
            return carry

        lax.fori_loop(0, heads, step, 0)
        ow_copy.wait()
        write_parts(nn(out_r[0], obuf[0]) + nn(out_r[1], obuf[1]), parts, rows)
        for h in range(max(0, heads - 2), heads):
            for c in out_copies(pbuf, (pa_o, pb_o), sems, h, h % 2):
                c.wait()

    probs = sds((heads, WINDOW, t), BF16)
    return call(
        body,
        [flags, *arrays],
        [sds((2, t, w), BF16), probs, probs] + [sds((rows, d), BF16)] * chunks,
        in_specs=[None] * (len(arrays) - 1) + ["hbm"],
        out_specs=[None, "hbm", "hbm"] + [None] * chunks,
        scratch=[
            pltpu.VMEM((2, 2, WINDOW, t), BF16),
            pltpu.SemaphoreType.DMA((2, 2)),
            pltpu.VMEM((2, w, d), BF16),
            pltpu.SemaphoreType.DMA((1,)),
        ],
        scalars=1,
        name=name,
        vmem=14,
    )


def score_back(p16, dp):
    p = p16.astype(F32)
    t = p * dp
    return (t - p * jnp.sum(t, axis=0, keepdims=True)).astype(BF16)


def distance_sums(ds):
    x = ds.astype(F32)
    n = WINDOW
    while n > 1:
        n //= 2
        x = x[:n] + pltpu.roll(x[n:], WINDOW - n, 1)
    return x


def attend_back(flags, q, selfs, cross, window, prev, pa, pb, branch, ow, adds, final, name):
    t, w = q.shape
    d = ow.shape[2]
    heads = w // HEAD_DIM
    count = len(branch)
    rows = t // count
    given = [a for a in adds if a is not None]
    arrays = [q, *selfs, *cross] + (list(prev) if prev else []) + [pa, pb, *branch, ow, *given]
    n_first = 7 if prev else 5

    def body(flags, *refs):
        refs = list(refs)
        q_r, ka_r, va_r, kb_r, vb_r = refs[:5]
        del refs[:5]
        if prev:
            kp_r, vp_r = refs.pop(0), refs.pop(0)
        pa_i, pb_i = refs.pop(0), refs.pop(0)
        br = refs[:count]
        ow_r = refs[count]
        del refs[: count + 1]
        add_refs = [None if a is None else refs.pop(0) for a in adds]
        dq_r, dka_r, dva_r, dkb_r, dvb_r = refs[:5]
        del refs[:5]
        if window:
            bd_r = refs.pop(0)
        if prev:
            dkp_r, dvp_r = refs.pop(0), refs.pop(0)
        do_r, pbuf, sems, obuf, osem = refs
        (ow_copy,) = fetch([(ow_r, obuf)], osem)
        flip = flags[FLIP]

        def loads(h, slot):
            return [pltpu.make_async_copy(p.at[h], pbuf.at[slot, k], sems.at[slot, k]) for k, p in enumerate((pa_i, pb_i))]

        for c in loads(0, 0):
            c.start()
        ow_copy.wait()
        for c in range(count):
            for k in range(2):
                do_r[k, c * rows : (c + 1) * rows, :] = nt(br[c][...], obuf[k]).astype(BF16)

        def step(h, carry):
            slot = h % 2
            at = lanes(h)

            @pl.when(h + 1 < heads)
            def _():
                for c in loads(h + 1, 1 - slot):
                    c.start()

            for c in loads(h, slot):
                c.wait()

            def put(ref, value, add):
                if add is not None:
                    value = value + add[:, at].astype(F32)
                ref[:, at] = value.astype(ref.dtype)

            qv, do_a, do_b = q_r[:, at], do_r[0, :, at], do_r[1, :, at]
            p16 = pbuf[slot, 0]
            dp = nt(va_r[:, at], do_a)
            if prev:
                key_row, query_row = window_masks(flip)
                tri = key_row <= query_row
                dp = jnp.where(tri, dp, nt(vp_r[:, at], do_a))
            ds = score_back(p16, dp)
            if window:
                bd_r[h] = distance_sums(ds)
            if prev:
                zero = jnp.zeros_like(ds)
                p_prev, ds_prev = jnp.where(tri, zero, p16), jnp.where(tri, zero, ds)
                p16, ds = jnp.where(tri, p16, zero), jnp.where(tri, ds, zero)
                dvp_r[:, at] = nn(p_prev, do_a)
                dkp_r[:, at] = nn(ds_prev, qv) * SCALE
            put(dva_r, nn(p16, do_a), add_refs[1])
            put(dka_r, nn(ds, qv) * SCALE, add_refs[0])
            dq = tn(ds, ka_r[:, at])
            if prev:
                dq = dq + tn(ds_prev, kp_r[:, at])
            p16 = pbuf[slot, 1]
            ds = score_back(p16, nt(vb_r[:, at], do_b))
            put(dvb_r, nn(p16, do_b), add_refs[3])
            put(dkb_r, nn(ds, qv) * SCALE, add_refs[2])
            dq = dq + tn(ds, kb_r[:, at])
            dq_r[:, at] = (dq * SCALE).astype(BF16)
            return carry

        lax.fori_loop(0, heads, step, 0)

    full = lambda dt: sds((t, w), dt)
    outs = [full(BF16), full(final[0]), full(final[0]), full(final[1]), full(final[1])]
    if window:
        outs.append(sds((heads, 1, WINDOW), F32))
    if prev:
        outs += [full(F32)] * 2
    return call(
        body,
        [flags, *arrays],
        outs,
        in_specs=[None] * n_first + ["hbm"] * 2 + [None] * count + ["hbm"] + [None] * len(given),
        scratch=[
            pltpu.VMEM((2, t, w), BF16),
            pltpu.VMEM((2, 2, WINDOW, t), BF16),
            pltpu.SemaphoreType.DMA((2, 2)),
            pltpu.VMEM((2, w, d), BF16),
            pltpu.SemaphoreType.DMA((1,)),
        ],
        scalars=1,
        name=name,
        vmem=14,
    )


def project_back(dq, dk, dv, wq, wk, wv, chunks, name):
    t, w = dq.shape
    d = wq.shape[0]
    rows = t // chunks

    def body(*refs):
        grads, weights, parts, bufs, sems = refs[:3], refs[3:6], refs[6:-4], refs[-4:-1], refs[-1]
        copies = fetch(zip(weights, bufs), sems)
        for c in copies:
            c.wait()
        for c, part in enumerate(parts):
            at = slice(c * rows, (c + 1) * rows)
            total = nt(grads[0][at, :], bufs[0][...])
            for g, buf in zip(grads[1:], bufs[1:]):
                total = total + nt(g[at, :], buf[...])
            part[...] = total.astype(BF16)

    return call(
        body,
        [dq, dk, dv, wq, wk, wv],
        [sds((rows, d), BF16)] * chunks,
        in_specs=[None] * 3 + ["hbm"] * 3,
        scratch=[pltpu.VMEM((d, w), BF16)] * 3 + [pltpu.SemaphoreType.DMA((3,))],
        name=name,
        vmem=10,
    )


def feed_forward(normed, cots, w_in, w_out, name):
    count = len(normed)
    rows, d = normed[0].shape
    f = w_in.shape[1]
    tile = min(f, 512)
    t = rows * count
    c0 = math.sqrt(2.0 / math.pi)

    def body(*refs):
        nm, og = refs[:count], refs[count : 2 * count]
        wi_r, wo_r, hid_r, pre_r = refs[2 * count : 2 * count + 4]
        rest = refs[2 * count + 4 :]
        parts_y, parts_g, (acc_y, acc_g, ibuf, obuf, sems) = rest[:count], rest[count : 2 * count], rest[-5:]

        def loads(i, slot):
            cols = pl.ds(pl.multiple_of(i * tile, tile), tile)
            return [
                pltpu.make_async_copy(wi_r.at[:, cols], ibuf.at[slot], sems.at[slot, 0]),
                pltpu.make_async_copy(wo_r.at[cols, :], obuf.at[slot], sems.at[slot, 1]),
            ]

        for c in loads(0, 0):
            c.start()
        acc_y[...] = jnp.zeros_like(acc_y)
        acc_g[...] = jnp.zeros_like(acc_g)

        def step(i, carry):
            cols = pl.ds(pl.multiple_of(i * tile, tile), tile)
            slot = i % 2

            @pl.when(i + 1 < f // tile)
            def _():
                for c in loads(i + 1, 1 - slot):
                    c.start()

            for c in loads(i, slot):
                c.wait()
            wi, wo = ibuf[slot], obuf[slot]
            for c in range(count):
                at = slice(c * rows, (c + 1) * rows)
                v = nn(nm[c][...], wi)
                sq = v * v
                th = jnp.tanh(v * (c0 + c0 * 0.044715 * sq))
                half = 0.5 + 0.5 * th
                hidden = (v * half).astype(BF16)
                slope = half + (0.5 * v) * (1.0 - th * th) * (c0 + 3.0 * c0 * 0.044715 * sq)
                hid_r[at, cols] = hidden
                pre = (nt(og[c][...], wo) * slope).astype(BF16)
                pre_r[at, cols] = pre
                acc_y[at, :] += nn(hidden, wo)
                acc_g[at, :] += nt(pre, wi)
            return carry

        lax.fori_loop(0, f // tile, step, 0)
        write_parts(acc_y, parts_y, rows)
        write_parts(acc_g, parts_g, rows)

    return call(
        body,
        [*normed, *cots, w_in, w_out],
        [sds((t, f), BF16)] * 2 + [sds((rows, d), BF16)] * (2 * count),
        in_specs=[None] * (2 * count) + ["hbm"] * 2,
        scratch=[pltpu.VMEM((t, d), F32)] * 2
        + [pltpu.VMEM((2, d, tile), BF16), pltpu.VMEM((2, tile, d), BF16), pltpu.SemaphoreType.DMA((2, 2))],
        name=name,
        vmem=18,
    )


def row_call(body, flags, arrays, outs, name, cost=0):
    n_in = len(arrays)

    def wrapped(flags, *refs):
        values = body(flags, *refs[:n_in])
        for o, v in zip(refs[n_in:], values):
            o[...] = jnp.sum(v, 0, keepdims=True) if o.shape[0] == 1 else v.astype(o.dtype)

    return call(wrapped, [flags, *arrays], outs, scalars=1, name=name, cost=cost)


def f32(ref):
    return ref[...].astype(F32)


def param(p_r, at):
    return p_r[at : at + 1, :]


def mid_norm(flags, tok, adds, params, name):
    def body(flags, tok_r, p_r, *adds_r):
        mid = f32(tok_r) + sum_refs(adds_r)
        return mid, norm_parts(mid)[0] * param(p_r, GAIN_MLP)

    return row_call(body, flags, [tok, params, *adds], [sds(tok.shape, F32), sds(tok.shape, BF16)], name)


def state_step(flags, first, second, adds, params, name):
    def body(flags, a_r, b_r, p_r, *adds_r):
        upd = sum_refs(adds_r)
        car = param(p_r, FORGET) * f32(a_r) + param(p_r, ADMIT) * upd
        st = jnp.where(flags[START].astype(F32) > 0.5, f32(b_r), car)
        return upd, car, st, norm_parts(st)[0] * param(p_r, GAIN_STATE)

    full = sds(first.shape, F32)
    arrays = [first, second, params, *adds]
    return row_call(body, flags, arrays, [full, full, full, sds(first.shape, BF16)], name)


def mid_back(flags, mid, params, cot, adds, name, cost=0):
    def body(flags, mid_r, p_r, cot_r, *adds_r):
        n, inv = norm_parts(mid_r[...])
        g = sum_refs(adds_r)
        mg = f32(cot_r) + norm_back(n, inv, param(p_r, GAIN_MLP), g)
        return mg, mg, g * n

    outs = [sds(mid.shape, F32), sds(mid.shape, BF16), sds((1, mid.shape[1]), F32)]
    return row_call(body, flags, [mid, params, cot, *adds], outs, name, cost)


def token_back(flags, live_at, tok, params, mg, cot, adds, name):
    def body(flags, tok_r, p_r, mg_r, cot_r, *adds_r):
        n, inv = norm_parts(f32(tok_r))
        g = sum_refs(adds_r)
        row = mg_r[...] + norm_back(n, inv, param(p_r, GAIN_TOK), g)
        if live_at is not None:
            row = jnp.where(flags[live_at].astype(F32) > 0.5, row, f32(cot_r))
        return row, g * n

    outs = [sds(tok.shape, F32), sds((1, tok.shape[1]), F32)]
    return row_call(body, flags, [tok, params, mg, cot, *adds], outs, name)


def gate_terms(snc, upd, state, p_r):
    sf, si = param(p_r, FORGET), param(p_r, ADMIT)
    return sf, si, snc * state * (sf * (1.0 - sf)), snc * upd * (si * (1.0 - si))


def state_back_second(flags, state, params, cot0, cot1, upd, adds, name):
    n_upd = len(upd)

    def body(flags, st_r, p_r, c0_r, c1_r, *rest):
        upd_v, adds_r = sum_refs(rest[:n_upd]), rest[n_upd:]
        live = flags[LIVE].astype(F32)
        start = flags[START].astype(F32)
        c0, c1 = f32(c0_r), f32(c1_r)
        snc = jnp.where(start > 0.5, c1, c0) * live
        st = st_r[...]
        n, inv = norm_parts(st)
        g = sum_refs(adds_r)
        sf, si, gf, gi = gate_terms(snc, upd_v, st, p_r)
        back = jnp.where(live > 0.5, sf * snc + norm_back(n, inv, param(p_r, GAIN_STATE), g), snc)
        snc0 = jnp.where(start > 0.5, c0, back)
        return jnp.where(start * live > 0.5, back, c1), snc0, si * snc0, g * n, gf, gi

    full, row = sds(state.shape, F32), sds((1, state.shape[1]), F32)
    arrays = [state, params, cot0, cot1, *upd, *adds]
    return row_call(body, flags, arrays, [full, full, sds(state.shape, BF16), row, row, row], name)


def state_back_first(flags, state, params, snc, upd, adds, name):
    def body(flags, st_r, p_r, snc_r, upd_r, *adds_r):
        st = f32(st_r)
        n, inv = norm_parts(st)
        g = sum_refs(adds_r)
        snc = snc_r[...]
        sf, _, gf, gi = gate_terms(snc, upd_r[...], st, p_r)
        return sf * snc + norm_back(n, inv, param(p_r, GAIN_STATE), g), g * n, gf, gi

    full, row = sds(state.shape, F32), sds((1, state.shape[1]), F32)
    arrays = [state, params, snc, upd, *adds]
    return row_call(body, flags, arrays, [full, row, row, row], name)


def piece_positions(index, size, order):
    rel = jnp.arange(size, dtype=jnp.int32) ^ index
    pos = jnp.zeros((size,), jnp.int32)
    for bit in order:
        pos = pos * 2 + ((rel >> bit) & 1)
    return pos


def weight_grads(table, jobs, size, name, cost=COVER):
    width = lambda a: a.shape[-1] * (2 if a.ndim == 3 else 1)
    first = lambda b: b[0] if isinstance(b, tuple) else b
    m = width(jobs[0][0][0])
    assert all(width(a) == m for lhs, _ in jobs for a in lhs)
    cols = [first(rhs[0][0]).shape[1] for _, rhs in jobs]
    n = sum(cols)
    tile = min([256] + [a.shape[-1] for lhs, _ in jobs for a in lhs])
    flat, plan = [], []

    def add(a):
        for k, b in enumerate(flat):
            if b is a:
                return k
        flat.append(a)
        return len(flat) - 1

    for lhs, rhs in jobs:
        parts = []
        for a, group in zip(lhs, rhs):
            at, row = add(a), 0
            for b in group:
                b, start, count = b if isinstance(b, tuple) else (b, 0, b.shape[0])
                parts.append((at, row, count, add(b), start))
                row += count
            assert row == a.shape[-2]
        plan.append(parts)
    shapes = [a.shape for a in flat]
    piece = m // size
    half = size // 2

    def body(*refs):
        table, refs = (None, refs) if len(refs) == len(flat) + 1 else (refs[0], refs[1:])

        def step(i, carry):
            col = 0
            for parts, width in zip(plan, cols):
                total = None
                for at, row, count, other, start in parts:
                    if len(shapes[at]) == 3:
                        blocks = shapes[at][2] // tile
                        here = pl.ds(pl.multiple_of((i % blocks) * tile, tile), tile)
                        a = refs[at][i // blocks, row : row + count, here]
                    else:
                        a = refs[at][row : row + count, pl.ds(pl.multiple_of(i * tile, tile), tile)]
                    term = tn(a, refs[other][start : start + count, :])
                    total = term if total is None else total + term
                out = total.astype(BF16)
                if table is None:
                    refs[-1][pl.ds(pl.multiple_of(i * tile, tile), tile), col : col + width] = out
                else:
                    keep, send = refs[-2:]
                    for j in range(tile // piece):
                        pos = table[i * (tile // piece) + j]
                        part = out[j * piece : (j + 1) * piece, :]

                        @pl.when(pos < half)
                        def _():
                            keep[pos, :, col : col + width] = part

                        @pl.when(pos >= half)
                        def _():
                            send[pos - half, :, col : col + width] = part

                col += width
            return carry

        lax.fori_loop(0, m // tile, step, 0)

    if table is None:
        outs = [sds((m, n), BF16)]
    else:
        outs = [sds((half, piece, n), BF16)] * 2
    args = flat if table is None else [table, *flat]
    return call(body, args, outs, scalars=len(args) - len(flat), name=name, vmem=12, cost=cost), cols


def split_rows(a, count):
    rows = a.shape[0] // count
    return [(a, k * rows, rows) for k in range(count)]


def widen(a, name):
    rows, n = a.shape
    tile = min(rows, 512)
    spec = pl.BlockSpec((tile, n), lambda i: (i, 0))

    def body(a_r, o_r):
        o_r[...] = a_r[...].astype(F32)

    return call(body, [a], [sds(a.shape, F32)], grid=(rows // tile,), in_specs=[spec], out_specs=[spec], name=name, vmem=28)[0]


def flip_dp(x, bit, size):
    return lax.ppermute(x, "dp", [(i, i ^ (1 << bit)) for i in range(size)])


def add_pair(a, b):
    return (a.astype(F32) + b.astype(F32)).astype(BF16)


def in_turn(x):
    return x if Order.last is None else after(x, Order.last)


def sum_pieces(pair, size, order):
    keep, send = pair
    got = flip_dp(send, order[0], size)
    yield
    for bit in order[1:]:
        half = keep.shape[0] // 2
        got = in_turn(got)
        keep, send = add_pair(keep[:half], got[:half]), add_pair(keep[half:], got[half:])
        Order.last = send
        got = flip_dp(send, bit, size)
        yield
    whole = add_pair(keep, in_turn(got))
    for bit in reversed(order[1:]):
        Order.last = whole
        got = flip_dp(whole, bit, size)
        yield
        whole = jnp.concatenate([whole, in_turn(got)], 0)
    Order.last = whole
    got = flip_dp(whole, order[0], size)
    yield
    yield whole, got


def sum_small(x, size, order):
    for bit in order:
        got = flip_dp(x, bit, size)
        yield
        x = x + in_turn(got)
        Order.last = x
    yield x


def place_pieces(table, own, other, widths, name):
    half, piece, n = own.shape
    size = 2 * half
    per = max(1, 256 // piece)

    def body(table, own_r, other_r, *outs):
        for j in range(per):
            pos = table[pl.program_id(0) * per + j]
            rows = slice(j * piece, (j + 1) * piece)

            def put(src, at):
                start = 0
                for o, width in zip(outs, widths):
                    o[rows, :] = src[at, :, start : start + width].astype(F32)
                    start += width

            @pl.when(pos < half)
            def _():
                put(own_r, pos)

            @pl.when(pos >= half)
            def _():
                put(other_r, pos - half)

    return call(
        body,
        [table, own, other],
        [sds((size * piece, width), F32) for width in widths],
        grid=(size // per,),
        in_specs=[pl.BlockSpec(own.shape, lambda i: (0, 0, 0), pipeline_mode=pl.Buffered(1))] * 2,
        out_specs=[pl.BlockSpec((per * piece, width), lambda i: (i, 0)) for width in widths],
        scalars=1,
        name=name,
        vmem=24,
    )


def local(
    head_size,
    dp_size,
    tokens,
    out_grad,
    init_state,
    state_grad,
    seq_blocks,
    bucket_table,
    gain_tok,
    gain_state,
    gain_mlp,
    query_tok,
    query_state,
    key_weight,
    value_weight,
    out_tok,
    out_state,
    mlp_in,
    mlp_out,
    gate_forget,
    gate_input,
    rel_bias,
):
    paired = head_size == 2
    chunks = 2 if paired else 1
    rows = tokens.shape[2]
    width = query_tok.shape[1]
    heads = width // HEAD_DIM

    def exchange(x):
        return lax.ppermute(x, "head", [(0, 1), (1, 0)])

    def gather(x):
        return (x, exchange(x)) if paired else (lax.all_gather(x, "head", axis=0, tiled=True),)

    def scatter(parts):
        if paired:
            return (parts[0], exchange(parts[1]))
        return (lax.psum_scatter(parts[0], "head", scatter_dimension=0, tiled=True),)

    first_len = seq_blocks[0, 0]
    live1 = (seq_blocks[0, 0] + seq_blocks[0, 1] > 1).astype(jnp.int32)
    start1 = (first_len == 1).astype(jnp.int32)
    flip = lax.axis_index("head") * rows if paired else jnp.int32(0)
    flags = jnp.stack([live1, start1, flip.astype(jnp.int32), 1 - start1])
    is_live, is_start = live1 > 0, start1 > 0

    onehot = (bucket_table[:, None] == jnp.arange(BUCKETS, dtype=jnp.int32)[None, :]).astype(F32)
    by_dist = jnp.dot(rel_bias.T, onehot.T, precision=lax.Precision.HIGHEST)[:, None, :]

    tok = [tokens[0, 0], tokens[0, 1]]
    init = [init_state[0, 0], init_state[0, 1]]
    cot = [out_grad[0, 0], out_grad[0, 1]]
    scot = [state_grad[0, 0], state_grad[0, 1]]
    live_cot = [cot[0], jnp.where(is_live, cot[1], jnp.zeros_like(cot[1]))]

    admit, forget = jax.nn.sigmoid(gate_input), jax.nn.sigmoid(gate_forget)
    bits = tuple(range(dp_size.bit_length() - 1))
    orders = (bits, bits[:1] + bits[2:] + bits[1:2])
    tables = [piece_positions(lax.axis_index("dp"), dp_size, order) for order in orders]
    add_all = lambda adds: functools.reduce(jnp.add, [a.astype(F32) for a in adds])
    hold = lambda parts, dep: [*parts[:-1], after(parts[-1], dep)]
    Order.last, Order.arrived = None, ()
    params = jnp.stack([gain_tok, gain_state, gain_mlp, forget, admit])
    params = jnp.concatenate([params, jnp.zeros((3, params.shape[1]), F32)], 0)

    def weight_sum(which, jobs, name):
        rows_of = lambda job: job[0][0].shape[-1] * (2 if job[0][0].ndim == 3 else 1)
        groups = {}
        for k, job in enumerate(jobs):
            groups.setdefault(rows_of(job), []).append(k)
        steps, cols = [], []
        for m, members in groups.items():
            pair, width = weight_grads(tables[which], [jobs[k] for k in members], dp_size, name)
            steps.append(sum_pieces(pair, dp_size, orders[which]))
            next(steps[-1])
            cols.append(width)
        return dict(steps=steps, which=which, cols=cols, members=list(groups.values()), name=name, pieces=None, grads=None)

    def advance(*sums):
        for w in sums:
            brought = [next(steps) for steps in w["steps"]]
            if brought[0] is not None:
                w["pieces"] = brought

    def place(w):
        grads = {}
        for members, pieces, cols in zip(w["members"], w["pieces"], w["cols"]):
            for k, grad in zip(members, place_pieces(tables[w["which"]], *pieces, cols, "pl_" + w["name"])):
                grads[k] = grad
        w["grads"] = [grads[k] for k in sorted(grads)]

    tok0_all, st0_all, tok1_all, cot1_all = gather(tok[0]), gather(init[0]), gather(tok[1]), gather(live_cot[1])
    nt0, qt0, kt0, vt0 = project(tok0_all, params, GAIN_TOK, query_tok, key_weight, value_weight, "proj_tok0")
    ns0, qs0, ks0, vs0 = project(st0_all, params, GAIN_STATE, query_state, key_weight, value_weight, "proj_state0")
    os0, pss0, psc0, *sparts = attend(
        flags, qs0, (ks0, vs0), (kt0, vt0), None, None, out_state, chunks, "att_state0"
    )
    sadds0 = scatter(sparts)
    nt1, qt1, kt1, vt1 = project(tok1_all, params, GAIN_TOK, query_tok, key_weight, value_weight, "proj_tok1")
    upd0, carried0, state1, sn1 = state_step(
        flags, init[0], init[1], sadds0, params, "state_step0"
    )
    sn1_all = gather(sn1)
    cot0_all = gather(after(live_cot[0], sn1))
    ot0, pts0, ptc0, *tparts = attend(
        flags, qt0, (kt0, vt0), (ks0, vs0), by_dist, None, out_tok, chunks, "att_tok0"
    )
    tadds0 = scatter(tparts)
    arrive(cot1_all)
    ns1, qs1, ks1, vs1 = project(sn1_all, params, None, query_state, key_weight, value_weight, "proj_state1")
    ot1, pts1, ptc1, *tparts = attend(
        flags, qt1, (kt1, vt1), (ks1, vs1), by_dist, (kt0, vt0), out_tok, chunks, "att_tok1"
    )
    tadds1 = scatter(tparts)
    mid0, nm0 = mid_norm(flags, tok[0], tadds0, params, "mid0")
    nm0_all = gather(nm0)
    arrive(cot0_all)
    os1, pss1, psc1, *sparts1 = attend(
        flags, qs1, (ks1, vs1), (kt1, vt1), None, None, out_state, chunks, "att_state1"
    )
    mid1, nm1 = mid_norm(flags, tok[1], tadds1, params, "mid1")
    nm1_all = gather(nm1)
    snc1 = jnp.where(is_start, scot[1], scot[0]).astype(F32) * live1.astype(F32)
    hid0, pre0, *mparts0 = feed_forward(nm0_all, cot0_all, mlp_in, mlp_out, "ff0")
    gadds0 = scatter(mparts0[chunks:])
    ug1_all = gather(after((admit * snc1).astype(BF16), hid0))
    hid1, pre1, *mparts1 = feed_forward(nm1_all, cot1_all, mlp_in, mlp_out, "ff1")
    gadds1 = scatter(mparts1[chunks:])

    (g_in,), _ = weight_grads(
        None, [([*nm0_all, *nm1_all], [[p] for p in split_rows(pre0, chunks) + split_rows(pre1, chunks)])], dp_size, "wg_in"
    )
    arrive(ug1_all)
    (g_out,), _ = weight_grads(None, [([hid0, hid1], [cot0_all, cot1_all])], dp_size, "wg_out", 0)
    d_in, d_out = lax.psum((g_in, g_out), "dp")
    mg1, mg16b, gm1 = mid_back(flags, mid1, params, live_cot[1], gadds1, "mid_back1")
    mg1_all = gather(mg16b)
    mg0, mg16, gm0 = mid_back(flags, mid0, params, live_cot[0], gadds0, "mid_back0")
    mg0_all = gather(mg16)
    dqs1, dks1, dvs1, dkt1, dvt1 = attend_back(
        flags, qs1, (ks1, vs1), (kt1, vt1), False, None, pss1, psc1, ug1_all, out_state, [None] * 4, (F32, F32), "att_state_back1"
    )
    sadds1 = scatter(hold(sparts1, dqs1))
    dqt1, dkt1, dvt1, dks1, dvs1, bd1, dkp, dvp = attend_back(
        flags, qt1, (kt1, vt1), (ks1, vs1), True, (kt0, vt0), pts1, ptc1, mg1_all, out_tok,
        [dkt1, dvt1, dks1, dvs1], (BF16, BF16), "att_tok_back1",
    )
    sback1 = project_back(dqs1, dks1, dvs1, query_state, key_weight, value_weight, chunks, "pb_state1")
    sback1 = scatter(sback1)
    dqt0, dkt0, dvt0, dks0, dvs0, bd0 = attend_back(
        flags, qt0, (kt0, vt0), (ks0, vs0), True, None, pts0, ptc0, mg0_all, out_tok,
        [dkp, dvp, None, None], (F32, F32), "att_tok_back0",
    )
    ig1, snc0, ug0, gs1, gf1, gi1 = state_back_second(
        flags, state1, params, scot[0], scot[1], sadds1, sback1, "state_back1"
    )
    ug0_all = gather(ug0)
    w_early = weight_sum(0, [([ot0, ot1], [mg0_all, mg1_all]), ([nt0, nt1], [[dqt0], [dqt1]])], "wg_early")
    madds0 = scatter(hold(mparts0[:chunks], ug0_all[-1]))
    madds1 = scatter(hold(mparts1[:chunks], ug0_all[-1]))
    dqs0, dks0, dvs0, dkt0, dvt0 = attend_back(
        flags, qs0, (ks0, vs0), (kt0, vt0), False, None, pss0, psc0, ug0_all, out_state,
        [dks0, dvs0, dkt0, dvt0], (BF16, BF16), "att_state_back0",
    )
    advance(w_early)
    sback0 = project_back(dqs0, dks0, dvs0, query_state, key_weight, value_weight, chunks, "pb_state0")
    sback0 = scatter(sback0)
    normed_all = [nt0, nt1, ns0, ns1]
    w_kv = weight_sum(
        0, [(normed_all, [[dkt0], [dkt1], [dks0], [dks1]]), (normed_all, [[dvt0], [dvt1], [dvs0], [dvs1]])], "wg_kv"
    )
    w_late = weight_sum(0, [([os0, os1], [ug0_all, ug1_all]), ([ns0, ns1], [[dqs0], [dqs1]])], "wg_late")
    advance(w_early, w_kv)
    arrive(madds0, madds1)
    tback0 = project_back(dqt0, dkt0, dvt0, query_tok, key_weight, value_weight, chunks, "pb_tok0")
    tback0 = scatter(tback0)
    tback1 = project_back(dqt1, dkt1, dvt1, query_tok, key_weight, value_weight, chunks, "pb_tok1")
    tback1 = scatter(tback1)
    advance(w_late)
    ig0, gs0, gf0, gi0 = state_back_first(
        flags, init[0], params, snc0, upd0, sback0, "state_back0"
    )
    row0, gt0 = token_back(flags, None, tok[0], params, mg0, cot[0], tback0, "tok_back0")
    row1, gt1 = token_back(flags, LIVE, tok[1], params, mg1, cot[1], tback1, "tok_back1")

    rel = jnp.dot((bd0 + bd1)[:, 0, :], onehot, precision=lax.Precision.HIGHEST)
    small = jnp.concatenate([gt0 + gt1, gs0 + gs1, gm0 + gm1, gf0 + gf1, gi0 + gi1], 0)
    small = small + exchange(small) if paired else lax.psum(small, "head")
    d = small.shape[1]
    rel_row = jnp.pad(rel.reshape(1, -1), ((0, 0), (0, d - heads * BUCKETS)))
    small = jnp.concatenate([small, rel_row, jnp.zeros((2, d), F32)], 0)
    w_small = dict(steps=[sum_small(small, dp_size, bits)], pieces=None)

    running = [w_early, w_kv, w_late, w_small]
    while running:
        advance(*running)
        for w in list(running):
            if w["pieces"] is not None:
                running.remove(w)
                if w is not w_small:
                    place(w)
    (d_ot, d_qt), (d_k, d_v), (d_os, d_qs) = w_early["grads"], w_kv["grads"], w_late["grads"]
    (small,) = w_small["pieces"]
    d_in, d_out = widen(d_in, "widen_in"), widen(d_out, "widen_out")
    d_rel = small[5, : heads * BUCKETS].reshape(heads, BUCKETS).T

    new0 = (mid0 + add_all(madds0)).astype(BF16)
    new1 = jnp.where(is_live, (mid1 + add_all(madds1)).astype(BF16), tok[1])
    carried1 = jnp.where(is_live, forget * state1 + admit * add_all(sadds1), state1)
    next0 = jnp.where(is_start, carried0, carried1)
    next1 = jnp.where(is_start & is_live, carried1, init[1].astype(F32))

    return (
        jnp.stack([new0, new1])[None],
        jnp.stack([next0, next1])[None],
        jnp.stack([row0, row1])[None],
        jnp.stack([ig0, ig1])[None],
        small[0],
        small[1],
        small[2],
        d_qt,
        d_qs,
        d_k,
        d_v,
        d_ot.reshape(out_tok.shape),
        d_os.reshape(out_state.shape),
        d_in,
        d_out,
        small[3],
        small[4],
        d_rel,
    )


def solution(mesh):
    rows = P("dp", None, "head", None)
    cols = P(None, "head")
    placed = (
        rows, rows, rows, rows, P("dp", None), P(), P(), P(), P(),
        cols, cols, cols, cols, P(None, "head", None), P(None, "head", None), cols, P("head", None),
        P(), P(), cols,
    )
    return jax.shard_map(
        functools.partial(local, mesh.shape["head"], mesh.shape["dp"]),
        mesh=mesh,
        in_specs=placed,
        out_specs=(
            rows, rows, rows, rows, P(), P(), P(),
            cols, cols, cols, cols, P(None, "head", None), P(None, "head", None), cols, P("head", None),
            P(), P(), cols,
        ),
        check_vma=False,
    )
```
